512 devices in a mesh: tile: 128 (over z, y, core), scan: 4 (over x).
Axes of the slice: x: 4, y: 4, z: 16, core: 2. Of those that a mesh axis runs over, the one named last changes fastest.
Arguments:
- object_slab: float32 [2, 2, 8192, 512], P(None, None, 'tile', 'scan'), may hold values from -6 to 6
- probe_wave: bfloat16 [2, 512, 512], P(None, None, 'scan'), may hold values from -6 to 6
- amplitudes: float32 [256, 512, 512], P('tile', 'scan'), may hold values from 0.2 to 2
- row_offsets: int32 [256], P('tile'), may hold values from 0 to 63
- position_counts: int32 [128], P('tile'), may hold values from 0 to 2, as said below
Outputs:
- object_grad: float32 [2, 2, 8192, 512], P(None, None, 'tile', 'scan')
The draws below stay inside these ranges and needn't reach their ends.
Inputs may be any that keep to these rules, and one draw needn't show every extreme that they name: position_counts is 1 to 2 on the first 120 tiles, equal to 2 on at least one of them, and 0 on the last 8 tiles.
All inputs are finite; a program needn't handle non-finite values.
Results may differ from the reference program's by a relative error of at most 0.0065.
Values may be sent and summed in bfloat16 or wider, within the bound.
A program may use at most 64 MiB of HBM per device.

```python
import math
import jax
import jax.numpy as jnp
from jax import lax

P_SIZE = 512
S = 2
TH = 64
POS_DEV = 2
TILES = 128
ROWS = 8192
NPOS = 256


def draw_position_counts(key, part):
    first_key, second_key = jax.random.split(jax.random.fold_in(key, 17))
    usable = TILES - P_SIZE // TH
    places = jnp.arange(TILES)
    counted = jax.random.randint(first_key, (TILES,), 1, POS_DEV + 1)
    busiest = jax.random.randint(second_key, (), 0, usable)
    counted = jnp.where(places == busiest, POS_DEV, counted)
    return jnp.where(places < usable, counted, 0).astype(jnp.int32)


def with_ends(values, own_key, low, top_value):
    index_at = [jax.random.randint(jax.random.fold_in(own_key, axis), (), 0, length) for axis, length in enumerate(values.shape)]
    widest = values.shape.index(max(values.shape))
    beside = index_at[:widest] + [(index_at[widest] + 1) % values.shape[widest]] + index_at[widest + 1:]
    return values.at[tuple(index_at)].set(low).at[tuple(beside)].set(top_value)


def block_scale(key, dims, shards, least, top_value):
    def one(axis_at, blocks):
        heights = jax.random.uniform(jax.random.fold_in(jax.random.fold_in(key, 6), axis_at), (blocks,), jnp.float32, least / len(shards), top_value / len(shards))
        return jnp.repeat(jnp.exp(heights), dims[axis_at] // blocks).reshape((-1,) + (1,) * (len(dims) - axis_at - 1))

    factor_of = one(*shards[0])
    for cut in shards[1:]:
        factor_of = factor_of * one(*cut)
    return factor_of


def bell_draw(key, shape, scale, limit, shards=(), kind=jnp.bfloat16):
    loudness = block_scale(key, shape, shards, -0.22, 0.18) if shards else 1.0
    entries = jax.random.normal(key, shape, jnp.float32) * scale * loudness
    return jnp.minimum(jnp.maximum(entries, -limit), limit).astype(kind)


def setup_inputs(seed: int = 0) -> dict:
    streams_of = jax.random.split(jax.random.key(seed), 6)
    object_slab = bell_draw(streams_of[0], (S, 2, ROWS, P_SIZE), 1.0, 6.0, ((2, 128), (3, 4)), jnp.float32)
    probe_wave = bell_draw(streams_of[1], (2, P_SIZE, P_SIZE), 1.0, 6.0, ((2, 4),))
    amplitudes = jnp.clip(0.2 + 1.8 * jax.random.uniform(streams_of[2], (NPOS, P_SIZE, P_SIZE), jnp.float32) ** block_scale(streams_of[2], (NPOS, P_SIZE, P_SIZE), ((0, 128), (1, 4)), -0.2, 0.2), 0.2, 2.0)
    row_offsets = with_ends(jax.random.randint(streams_of[3], (NPOS,), 0, TH), jax.random.fold_in(streams_of[3], 1), 0, TH - 1).astype(jnp.int32)
    position_counts = draw_position_counts(jax.random.fold_in(streams_of[5], 71), 0)
    return dict(object_slab=object_slab, probe_wave=probe_wave, amplitudes=amplitudes, row_offsets=row_offsets, position_counts=position_counts)


fresnel = 0.5
smooth = 1.0

def tables():
    index = jnp.arange(P_SIZE, dtype=jnp.int32)
    modded = index[:, None] * index[None, :] % P_SIZE
    angles = 2.0 * jnp.pi / P_SIZE * modded.astype(jnp.float32)
    cosine = jnp.cos(angles)
    sine_table = jnp.sin(angles)
    scaling = 1.0 / math.sqrt(P_SIZE)
    far_table = jnp.stack([cosine * scaling, -sine_table * scaling]).astype(jnp.bfloat16)
    centred = jnp.where(index < P_SIZE // 2, index, index - P_SIZE).astype(jnp.float32)
    phases = -jnp.pi * fresnel / P_SIZE * centred * centred
    kernel_real = jnp.cos(phases)
    kernel_imag = jnp.sin(phases)
    scaled_real = cosine * kernel_real[None, :] - sine_table * kernel_imag[None, :]
    scaled_imag = cosine * kernel_imag[None, :] + sine_table * kernel_real[None, :]
    highest = lax.Precision.HIGHEST
    fresnel_real = (jnp.dot(scaled_real, cosine, precision=highest) + jnp.dot(scaled_imag, sine_table, precision=highest)) / P_SIZE
    fresnel_imag = (jnp.dot(scaled_imag, cosine, precision=highest) - jnp.dot(scaled_real, sine_table, precision=highest)) / P_SIZE
    return (far_table, jnp.stack([fresnel_real, fresnel_imag]).astype(jnp.bfloat16))

def product(left, right):
    return jnp.dot(left.astype(jnp.float32), right.astype(jnp.float32), preferred_element_type=jnp.float32)

def left_apply(table, conjugate, real_part, imaginary):
    table_real = table[0]
    table_imag = -table[1] if conjugate else table[1]
    return (product(table_real, real_part) - product(table_imag, imaginary), product(table_real, imaginary) + product(table_imag, real_part))

def right_apply(table, conjugate, real_part, imaginary):
    table_real = table[0]
    table_imag = -table[1] if conjugate else table[1]
    return (product(real_part, table_real) - product(imaginary, table_imag), product(real_part, table_imag) + product(imaginary, table_real))

def halves(pair):
    return (pair[0].astype(jnp.bfloat16), pair[1].astype(jnp.bfloat16))

def position_terms(patch, probe_wave, measured, far_table, fresnel_table):
    single = jnp.float32
    first_real = patch[0, 0].astype(single)
    first_imag = patch[0, 1].astype(single)
    second_real = patch[1, 0].astype(single)
    second_imag = patch[1, 1].astype(single)
    probe_real = probe_wave[0].astype(single)
    probe_imag = probe_wave[1].astype(single)
    psi_one = halves((probe_real * first_real - probe_imag * first_imag, probe_real * first_imag + probe_imag * first_real))
    half_one = halves(left_apply(fresnel_table, False, psi_one[0], psi_one[1]))
    psi_two = halves(right_apply(fresnel_table, False, half_one[0], half_one[1]))
    wave_real = psi_two[0].astype(single)
    wave_imag = psi_two[1].astype(single)
    exit_wave = halves((wave_real * second_real - wave_imag * second_imag, wave_real * second_imag + wave_imag * second_real))
    half_two = halves(left_apply(far_table, False, exit_wave[0], exit_wave[1]))
    field_real, field_imag = right_apply(far_table, False, half_two[0], half_two[1])
    modulus = jnp.sqrt(field_real * field_real + field_imag * field_imag + smooth)
    keeping = 1.0 - measured / modulus
    chi_wave = halves((field_real * keeping, field_imag * keeping))
    back_one = halves(right_apply(far_table, True, chi_wave[0], chi_wave[1]))
    exit_real, exit_imag = left_apply(far_table, True, back_one[0], back_one[1])
    term_two = jnp.stack([wave_real * exit_real + wave_imag * exit_imag, wave_real * exit_imag - wave_imag * exit_real])
    grad_wave = halves((second_real * exit_real + second_imag * exit_imag, second_real * exit_imag - second_imag * exit_real))
    back_two = halves(right_apply(fresnel_table, True, grad_wave[0], grad_wave[1]))
    enter_real, enter_imag = left_apply(fresnel_table, True, back_two[0], back_two[1])
    term_one = jnp.stack([probe_real * enter_real + probe_imag * enter_imag, probe_real * enter_imag - probe_imag * enter_real])
    return jnp.stack([term_one, term_two])

def reference(object_slab, probe_wave, amplitudes, row_offsets, position_counts):
    far_table, fresnel_table = tables()
    slab_half = object_slab.astype(jnp.bfloat16)
    total = jnp.zeros(object_slab.shape, jnp.float32)

    def visit(position, total):
        position = jnp.asarray(position).astype(jnp.int32)
        home_tile = position // POS_DEV
        slot_index = position % POS_DEV
        start = (home_tile * TH + row_offsets[position]).astype(jnp.int32)

        def update(total):
            patch = lax.dynamic_slice_in_dim(slab_half, start, P_SIZE, 2)
            terms = position_terms(patch, probe_wave, amplitudes[position], far_table, fresnel_table)
            current = lax.dynamic_slice_in_dim(total, start, P_SIZE, 2)
            return lax.dynamic_update_slice_in_dim(total, current + terms, start, 2)

        def unchanged(total):
            return total
        return lax.cond(slot_index < position_counts[home_tile], update, unchanged, total)
    return lax.fori_loop(0, NPOS, visit, total)
```

```python
import functools
import math

import jax
import jax.numpy as jnp
import numpy as np
from jax import lax
from jax.experimental import pallas as pl
from jax.experimental.pallas import tpu as pltpu
from jax.sharding import PartitionSpec as P

P_SIZE = 512
HALF = 256
BLK = 128
TH = 64
SPAN = P_SIZE // TH

fresnel = 0.5
smooth = 1.0
MESH = pl.DeviceIdType.MESH
BF = jnp.bfloat16
F32 = jnp.float32


def tables():
    index = np.arange(P_SIZE)
    angles = 2.0 * np.pi / P_SIZE * (index[:, None] * index[None, :] % P_SIZE)
    wave = np.exp(1j * angles)
    far = np.conj(wave) / math.sqrt(P_SIZE)
    centred = np.where(index < P_SIZE // 2, index, index - P_SIZE).astype(np.float64)
    kernel = np.exp(-1j * np.pi * fresnel / P_SIZE * centred * centred)
    near = (wave * kernel[None, :]) @ np.conj(wave).T / P_SIZE

    def planes(table):
        both = np.stack([table.real, table.imag])
        return both.astype(np.float32).astype(BF)

    return planes(far), planes(near)


def body(
    tiles,
    off_ref, cnt_ref, slab_hbm, probe_hbm, amp_hbm, tq_hbm, tf_hbm,
    out_ref,
    slab, probe, ampf, aq, bq, af, bf,
    stage, win, sel, put, h1, o2p, ampb, hr, o2r, amp,
    ps, ew, gs, x1, ch, ks, y, t2s, gw, b2s, b2r, t2r, tp, outs, oin,
    loc_sem, tab_sem,
    in_ss, in_rs, h1_ss, h1_rs, o2_ss, o2_rs, am_ss, am_rs,
    e1_ss, e1_rs, e2_ss, e2_rs, b2_ss, b2_rs, t2_ss, t2_rs, out_ss, out_rs,
):
    t = lax.axis_index("tile")
    x = lax.axis_index("scan")
    c = lax.rem(t, 2)
    d = 1 - c
    pair = t - c
    home = pair + x // 2
    slot = lax.rem(x, 2)

    def remote(src, dst, ss, rs, tile, scan):
        return pltpu.make_async_remote_copy(
            src_ref=src, dst_ref=dst, send_sem=ss, recv_sem=rs,
            device_id={"tile": tile, "scan": scan}, device_id_type=MESH,
        )

    barrier = pltpu.get_barrier_semaphore()

    def greet(tile, scan):
        pl.semaphore_signal(
            barrier, inc=1, device_id={"tile": tile, "scan": scan}, device_id_type=MESH
        )

    for k in range(1, SPAN + 1):
        greet(lax.rem(t + k, tiles), x)
        greet(lax.rem(t + tiles - k, tiles), x)
    for step in range(1, 4):
        for core in range(2):
            greet(pair + core, lax.rem(x + step, 4))

    loads = [
        pltpu.make_async_copy(slab_hbm, slab, loc_sem.at[0]),
        pltpu.make_async_copy(amp_hbm, ampf, loc_sem.at[1]),
        pltpu.make_async_copy(probe_hbm, probe, loc_sem.at[2]),
    ]
    for load in loads:
        load.start()

    def table_loads(src, dst, which, column):
        copies = []
        for n, (up, left, plane) in enumerate([(0, 0, 0), (1 - column, column, 1), (1, 1, 0)]):
            where = dst.at[pl.ds(up * P_SIZE, P_SIZE), pl.ds(left * P_SIZE, P_SIZE)]
            copies.append(pltpu.make_async_copy(src.at[plane], where, tab_sem.at[which, n]))
        for copy in copies:
            copy.start()
        return copies

    def table_ready(dst, copies, column):
        for copy in copies:
            copy.wait()
        imag = dst[(1 - column) * P_SIZE:(2 - column) * P_SIZE, column * P_SIZE:(column + 1) * P_SIZE]
        dst[column * P_SIZE:(column + 1) * P_SIZE, (1 - column) * P_SIZE:(2 - column) * P_SIZE] = -imag

    aq_loads = table_loads(tq_hbm, aq, 0, 0)
    bq_loads = table_loads(tq_hbm, bq, 1, 1)
    bf_loads = table_loads(tf_hbm, bf, 2, 1)
    af_loads = table_loads(tf_hbm, af, 3, 0)

    loads[0].wait()
    for s in range(2):
        for part in range(2):
            piece = slab[s, part].astype(BF)
            stage[s, :, part * BLK:(part + 1) * BLK] = piece
            win[s, 0, :, part * BLK:(part + 1) * BLK] = piece
    loads[1].wait()
    for s in range(2):
        for r in range(2):
            ampb[s, r] = ampf[s, :, r * HALF:(r + 1) * HALF].astype(BF)
    for s in range(2):
        shape = (P_SIZE, P_SIZE + TH)
        shifted = lax.broadcasted_iota(jnp.int32, shape, 0) + off_ref[s]
        match = shifted == lax.broadcasted_iota(jnp.int32, shape, 1)
        sel[s] = jnp.where(match, 1.0, 0.0).astype(BF)
        shape = (P_SIZE + TH, P_SIZE)
        shifted = lax.broadcasted_iota(jnp.int32, shape, 1) + off_ref[s]
        match = shifted == lax.broadcasted_iota(jnp.int32, shape, 0)
        alive = jnp.broadcast_to(cnt_ref[0], shape) > s
        put[:, s * P_SIZE:(s + 1) * P_SIZE] = jnp.where(
            jnp.logical_and(match, alive), 1.0, 0.0).astype(BF)

    pl.semaphore_wait(barrier, 2 * SPAN + 6)

    sends = []
    for s in range(2):
        for k in range(1, SPAN + 1):
            copy = remote(
                stage.at[s], win.at[s, k], in_ss.at[s, k], in_rs.at[s, k],
                lax.rem(t + tiles - k, tiles), x,
            )
            copy.start()
            sends.append(copy)

    def is_self(s, r):
        return jnp.logical_and(2 * c + s == x, c == r)

    def spread(src, dst, ss, rs, s, r):
        mine = is_self(s, r)

        @pl.when(mine)
        def _():
            pltpu.make_async_copy(src, dst.at[x], rs.at[x]).start()

        @pl.when(jnp.logical_not(mine))
        def _():
            remote(src, dst.at[x], ss.at[s, r], rs.at[x], pair + r, 2 * c + s).start()

    def spread_wait(src, dst, ss, rs, s, r):
        @pl.when(jnp.logical_not(is_self(s, r)))
        def _():
            remote(src, dst.at[x], ss.at[s, r], rs.at[x], pair + r, 2 * c + s).wait_send()

    def amp_of(s, r):
        return ampb.at[s, r], amp, am_ss, am_rs, s, r

    def h1_of(s, r):
        return h1.at[s, :, pl.ds(r * HALF, HALF), :], hr, h1_ss, h1_rs, s, r

    def o2_of(s, r):
        return o2p.at[s, :, pl.ds(r * HALF, HALF), :], o2r, o2_ss, o2_rs, s, r

    for s in range(2):
        for r in range(2):
            spread(*amp_of(s, r))

    table_ready(aq, aq_loads, 0)
    table_ready(bq, bq_loads, 1)
    table_ready(bf, bf_loads, 1)
    table_ready(af, af_loads, 0)

    def receive(dst, rs):
        pltpu.make_async_copy(dst, dst, rs).wait()

    def window(s):
        for k in range(1, SPAN + 1):
            receive(win.at[s, k], in_rs.at[s, k])
        return jnp.concatenate([win[s, k] for k in range(SPAN + 1)], axis=0)

    def dot(left, right):
        return jnp.dot(left, right, preferred_element_type=F32)

    loads[2].wait()
    wide = window(0)
    psi = []
    for s in range(2):
        patch = dot(sel[s], wide)
        pr, pi = probe[0].astype(F32), probe[1].astype(F32)
        fr, fi = patch[:, :BLK], patch[:, BLK:]
        psi.append(jnp.concatenate([
            (pr * fr - pi * fi).astype(BF), (pr * fi + pi * fr).astype(BF)], axis=0))
    psi = jnp.concatenate(psi, axis=1)
    for r in range(2):
        for part in range(2):
            at = part * P_SIZE + r * HALF
            half1 = dot(aq[at:at + HALF, :], psi).astype(BF)
            for s in range(2):
                h1[s, part, r * HALF:(r + 1) * HALF, :] = half1[:, s * BLK:(s + 1) * BLK]
        for s in range(2):
            spread(*h1_of(s, r))

    wide = window(1)
    for s in range(2):
        patch = dot(sel[s], wide).astype(BF)
        for part in range(2):
            o2p[s, part] = patch[:, part * BLK:(part + 1) * BLK]
        for r in range(2):
            spread(*o2_of(s, r))

    for n in range(4):
        receive(hr.at[n], h1_rs.at[n])
    left = jnp.concatenate([hr[n, part] for part in range(2) for n in range(4)], axis=1)
    for part in range(2):
        for h in range(2):
            at = part * P_SIZE + h * HALF
            ps[part, h] = dot(left, bq[:, at:at + HALF]).astype(BF)
    for n in range(4):
        receive(o2r.at[n], o2_rs.at[n])

    def second(part, h):
        return jnp.concatenate([o2r[2 * h, part], o2r[2 * h + 1, part]], axis=1).astype(F32)

    for h in range(2):
        wr, wi = ps[0, h].astype(F32), ps[1, h].astype(F32)
        sr, si = second(0, h), second(1, h)
        ew[:, h * HALF:(h + 1) * HALF] = (wr * sr - wi * si).astype(BF)
        ew[:, P_SIZE + h * HALF:P_SIZE + (h + 1) * HALF] = (wr * si + wi * sr).astype(BF)

    for part in range(2):
        at = pl.multiple_of(part * P_SIZE + d * HALF, HALF)
        gs[part] = dot(ew[...], bf[:, pl.ds(at, HALF)]).astype(BF)
    ex1 = remote(gs, x1.at[c], e1_ss, e1_rs, pair + d, x)
    ex1.start()
    for part in range(2):
        at = pl.multiple_of(part * P_SIZE + c * HALF, HALF)
        x1[c, part] = dot(ew[...], bf[:, pl.ds(at, HALF)]).astype(BF)
    for n in range(4):
        receive(amp.at[n], am_rs.at[n])
    receive(x1.at[d], e1_rs)

    right = jnp.concatenate([x1[r, part] for part in range(2) for r in range(2)], axis=0)
    for r in range(2):
        fr = dot(af[r * HALF:(r + 1) * HALF, :], right)
        fi = dot(af[P_SIZE + r * HALF:P_SIZE + (r + 1) * HALF, :], right)
        measured = jnp.concatenate([amp[2 * r], amp[2 * r + 1]], axis=0).astype(F32)
        keeping = 1.0 - measured / jnp.sqrt(fr * fr + fi * fi + smooth)
        ch[r * HALF:(r + 1) * HALF, :] = (fr * keeping).astype(BF)
        ch[P_SIZE + r * HALF:P_SIZE + (r + 1) * HALF, :] = (fi * keeping).astype(BF)

    for part in range(2):
        at = pl.multiple_of(part * P_SIZE + d * HALF, HALF)
        ks[part] = dot(bf[pl.ds(at, HALF), :], ch[...]).astype(BF)
    ex2 = remote(ks, y.at[c], e2_ss, e2_rs, pair + d, x)
    ex2.start()
    for part in range(2):
        at = pl.multiple_of(part * P_SIZE + c * HALF, HALF)
        y[c, part] = dot(bf[pl.ds(at, HALF), :], ch[...]).astype(BF)
    receive(y.at[d], e2_rs)

    left = jnp.concatenate([y[h, part] for part in range(2) for h in range(2)], axis=1)
    for h in range(2):
        er = dot(left, af[:, h * HALF:(h + 1) * HALF])
        ei = dot(left, af[:, P_SIZE + h * HALF:P_SIZE + (h + 1) * HALF])
        wr, wi = ps[0, h].astype(F32), ps[1, h].astype(F32)
        sr, si = second(0, h), second(1, h)
        tr, ti = (wr * er + wi * ei).astype(BF), (wr * ei - wi * er).astype(BF)
        for n in range(2):
            t2s[2 * h + n, 0] = tr[:, n * BLK:(n + 1) * BLK]
            t2s[2 * h + n, 1] = ti[:, n * BLK:(n + 1) * BLK]
        gw[:, h * HALF:(h + 1) * HALF] = (sr * er + si * ei).astype(BF)
        gw[:, P_SIZE + h * HALF:P_SIZE + (h + 1) * HALF] = (sr * ei - si * er).astype(BF)

    def is_home(n):
        return jnp.logical_and(home == t, x == n)

    def give(src, dst, ss, rs, n):
        where = dst.at[slot, :, pl.ds(pl.multiple_of(c * HALF, HALF), HALF), :]

        @pl.when(is_home(n))
        def _():
            pltpu.make_async_copy(src.at[n], where, rs.at[slot, c]).start()

        @pl.when(jnp.logical_not(is_home(n)))
        def _():
            remote(src.at[n], where, ss.at[n], rs.at[slot, c], home, n).start()

    def give_wait(src, dst, ss, rs, n):
        where = dst.at[slot, :, pl.ds(pl.multiple_of(c * HALF, HALF), HALF), :]

        @pl.when(jnp.logical_not(is_home(n)))
        def _():
            remote(src.at[n], where, ss.at[n], rs.at[slot, c], home, n).wait_send()

    for h in range(2):
        for part in range(2):
            at = part * P_SIZE + h * HALF
            back2 = dot(gw[...], aq[:, at:at + HALF]).astype(BF)
            for n in range(2):
                b2s[2 * h + n, part] = back2[:, n * BLK:(n + 1) * BLK]
        for n in range(2):
            give(b2s, b2r, b2_ss, b2_rs, 2 * h + n)
    for n in range(4):
        give(t2s, t2r, t2_ss, t2_rs, n)

    for s in range(2):
        for r in range(2):
            receive(b2r.at[s, :, pl.ds(r * HALF, HALF), :], b2_rs.at[s, r])
    right = jnp.concatenate([
        jnp.concatenate([b2r[0, part], b2r[1, part]], axis=1) for part in range(2)], axis=0)
    for r in range(2):
        nr = dot(bq[r * HALF:(r + 1) * HALF, :], right)
        ni = dot(bq[P_SIZE + r * HALF:P_SIZE + (r + 1) * HALF, :], right)
        pr = probe[0, r * HALF:(r + 1) * HALF, :].astype(F32)
        pi = probe[1, r * HALF:(r + 1) * HALF, :].astype(F32)
        for s in range(2):
            sr, si = nr[:, s * BLK:(s + 1) * BLK], ni[:, s * BLK:(s + 1) * BLK]
            rows = slice(s * P_SIZE + r * HALF, s * P_SIZE + (r + 1) * HALF)
            tp[rows, :BLK] = (pr * sr + pi * si).astype(BF)
            tp[rows, BLK:] = (pr * si - pi * sr).astype(BF)

    def collect(which, terms):
        for first, last in ((1, 5), (5, 9), (0, 1)):
            total = dot(put[first * TH:last * TH, :], terms)
            if first == 0:
                for part in range(2):
                    out_ref[which, part] = total[:, part * BLK:(part + 1) * BLK]
                continue
            for k in range(first, last):
                outs[which, k] = total[(k - first) * TH:(k - first + 1) * TH].astype(BF)
                copy = remote(
                    outs.at[which, k], oin.at[which, k], out_ss.at[which, k],
                    out_rs.at[which, k], lax.rem(t + k, tiles), x,
                )
                copy.start()
                sends.append(copy)

    collect(0, tp[...])
    for s in range(2):
        for r in range(2):
            receive(t2r.at[s, :, pl.ds(r * HALF, HALF), :], t2_rs.at[s, r])
    terms = jnp.concatenate([
        jnp.concatenate([t2r[s, part] for part in range(2)], axis=1) for s in range(2)], axis=0)
    collect(1, terms)

    for which in range(2):
        for k in range(1, SPAN + 1):
            receive(oin.at[which, k], out_rs.at[which, k])
        for part in range(2):
            total = out_ref[which, part]
            for k in range(1, SPAN + 1):
                total = total + oin[which, k, :, part * BLK:(part + 1) * BLK].astype(F32)
            out_ref[which, part] = total

    for copy in sends:
        copy.wait_send()
    ex1.wait_send()
    ex2.wait_send()
    for s in range(2):
        for r in range(2):
            spread_wait(*amp_of(s, r))
            spread_wait(*h1_of(s, r))
            spread_wait(*o2_of(s, r))
    for n in range(4):
        give_wait(b2s, b2r, b2_ss, b2_rs, n)
        give_wait(t2s, t2r, t2_ss, t2_rs, n)


def shards(tiles, far, near, object_slab, probe_wave, amplitudes, row_offsets, position_counts):
    dma = pltpu.SemaphoreType.DMA
    vmem = pltpu.VMEM
    n2 = 2 * P_SIZE
    scratch = [
        vmem((2, 2, TH, BLK), F32),
        vmem((2, P_SIZE, BLK), BF),
        vmem((2, BLK, P_SIZE), F32),
        vmem((n2, n2), BF), vmem((n2, n2), BF), vmem((n2, n2), BF), vmem((n2, n2), BF),
        vmem((2, TH, HALF), BF),
        vmem((2, SPAN + 1, TH, HALF), BF),
        vmem((2, P_SIZE, P_SIZE + TH), BF),
        vmem((P_SIZE + TH, n2), BF),
        vmem((2, 2, P_SIZE, BLK), BF),
        vmem((2, 2, P_SIZE, BLK), BF),
        vmem((2, 2, BLK, HALF), BF),
        vmem((4, 2, HALF, BLK), BF),
        vmem((4, 2, HALF, BLK), BF),
        vmem((4, BLK, HALF), BF),
        vmem((2, 2, HALF, HALF), BF),
        vmem((HALF, n2), BF),
        vmem((2, HALF, HALF), BF),
        vmem((2, 2, HALF, HALF), BF),
        vmem((n2, HALF), BF),
        vmem((2, HALF, HALF), BF),
        vmem((2, 2, HALF, HALF), BF),
        vmem((4, 2, HALF, BLK), BF),
        vmem((HALF, n2), BF),
        vmem((4, 2, HALF, BLK), BF),
        vmem((2, 2, P_SIZE, BLK), BF),
        vmem((2, 2, P_SIZE, BLK), BF),
        vmem((n2, HALF), BF),
        vmem((2, SPAN + 1, TH, HALF), BF),
        vmem((2, SPAN + 1, TH, HALF), BF),
        dma((3,)), dma((4, 3)),
        dma((2, SPAN + 1)), dma((2, SPAN + 1)),
        dma((2, 2)), dma((4,)), dma((2, 2)), dma((4,)), dma((2, 2)), dma((4,)),
        dma, dma, dma, dma,
        dma((4,)), dma((2, 2)), dma((4,)), dma((2, 2)),
        dma((2, SPAN + 1)), dma((2, SPAN + 1)),
    ]
    any_spec = pl.BlockSpec(memory_space=pl.ANY)
    smem_spec = pl.BlockSpec(memory_space=pltpu.SMEM)
    return pl.pallas_call(
        functools.partial(body, tiles),
        out_shape=jax.ShapeDtypeStruct(object_slab.shape, F32),
        in_specs=[smem_spec, smem_spec] + [any_spec] * 5,
        out_specs=pl.BlockSpec(memory_space=pltpu.VMEM),
        scratch_shapes=scratch,
        compiler_params=pltpu.CompilerParams(
            collective_id=0, has_side_effects=True, vmem_limit_bytes=48 * 1024 * 1024
        ),
        name="object_gradient",
    )(row_offsets, position_counts, object_slab, probe_wave, amplitudes, near, far)


def solution(mesh):
    in_specs = (
        P(None, None, "tile", "scan"),
        P(None, None, "scan"),
        P("tile", "scan", None),
        P("tile"),
        P("tile"),
    )
    out_specs = P(None, None, "tile", "scan")
    far, near = tables()
    run = functools.partial(shards, mesh.shape["tile"], far, near)
    return jax.shard_map(run, mesh=mesh, in_specs=in_specs, out_specs=out_specs, check_vma=False)
```

```python
import functools
import math

import jax
import jax.numpy as jnp
import numpy as np
from jax import lax
from jax.experimental import pallas as pl
from jax.experimental.pallas import tpu as pltpu
from jax.sharding import PartitionSpec as P

P_SIZE = 512
HALF = 256
BLK = 128
TH = 64
SPAN = P_SIZE // TH

fresnel = 0.5
smooth = 1.0
MESH = pl.DeviceIdType.MESH
BF = jnp.bfloat16
F32 = jnp.float32


def tables():
    index = np.arange(P_SIZE)
    angles = 2.0 * np.pi / P_SIZE * (index[:, None] * index[None, :] % P_SIZE)
    wave = np.exp(1j * angles)
    far = np.conj(wave) / math.sqrt(P_SIZE)
    centred = np.where(index < P_SIZE // 2, index, index - P_SIZE).astype(np.float64)
    kernel = np.exp(-1j * np.pi * fresnel / P_SIZE * centred * centred)
    near = (wave * kernel[None, :]) @ np.conj(wave).T / P_SIZE

    def planes(table):
        both = np.stack([table.real, table.imag])
        return both.astype(np.float32).astype(BF)

    return planes(far), planes(near)


def body(
    tiles,
    off_hbm, cnt_hbm, slab_hbm, probe_hbm, amp_hbm, tq_hbm, tf_hbm,
    out_ref,
    off_ref, cnt_ref, slab, probe, ampf, aq, bq, af, bf,
    win, sel, put, h1, o2p, ampb, hr, o2r, amp,
    ps, ew, gs, x1, ch, ks, y, t2s, gw, b2s, b2r, t2r, tp, odd, got, even, outs, oin,
    loc_sem, tab_sem,
    in_ss, in_rs, fw_ss, h1_ss, h1_rs, o2_ss, o2_rs, am_ss, am_rs,
    e1_ss, e1_rs, e2_ss, e2_rs, b2_ss, b2_rs, t2_ss, t2_rs, od_ss, od_rs, out_ss, out_rs,
):
    t = lax.axis_index("tile")
    x = lax.axis_index("scan")
    c = lax.rem(t, 2)
    d = 1 - c
    pair = t - c
    home = pair + lax.rem(x, 2)
    slot = x // 2

    def remote(src, dst, ss, rs, tile, scan):
        return pltpu.make_async_remote_copy(
            src_ref=src, dst_ref=dst, send_sem=ss, recv_sem=rs,
            device_id={"tile": tile, "scan": scan}, device_id_type=MESH,
        )

    loads = [
        pltpu.make_async_copy(slab_hbm, slab, loc_sem.at[0]),
        pltpu.make_async_copy(amp_hbm, ampf, loc_sem.at[1]),
        pltpu.make_async_copy(probe_hbm, probe, loc_sem.at[2]),
        pltpu.make_async_copy(off_hbm, off_ref, loc_sem.at[3]),
        pltpu.make_async_copy(cnt_hbm, cnt_ref, loc_sem.at[4]),
    ]
    for load in loads:
        load.start()

    barrier = pltpu.get_barrier_semaphore()

    def greet(tile, scan):
        pl.semaphore_signal(
            barrier, inc=1, device_id={"tile": tile, "scan": scan}, device_id_type=MESH
        )

    greet(pair + d, x)
    for k in range(2, SPAN + 1, 2):
        greet(lax.rem(t + k, tiles), x)
        greet(lax.rem(t + tiles - k, tiles), x)
    for step in range(1, 4):
        for core in range(2):
            greet(pair + core, lax.rem(x + step, 4))

    def table_loads(src, dst, which, column):
        copies = []
        for n, (up, left, plane) in enumerate([(0, 0, 0), (1 - column, column, 1), (1, 1, 0)]):
            where = dst.at[pl.ds(up * P_SIZE, P_SIZE), pl.ds(left * P_SIZE, P_SIZE)]
            copies.append(pltpu.make_async_copy(src.at[plane], where, tab_sem.at[which, n]))
        for copy in copies:
            copy.start()
        return copies

    def table_ready(dst, copies, column):
        for copy in copies:
            copy.wait()
        imag = dst[(1 - column) * P_SIZE:(2 - column) * P_SIZE, column * P_SIZE:(column + 1) * P_SIZE]
        dst[column * P_SIZE:(column + 1) * P_SIZE, (1 - column) * P_SIZE:(2 - column) * P_SIZE] = -imag

    aq_loads = table_loads(tq_hbm, aq, 0, 0)
    bq_loads = table_loads(tq_hbm, bq, 1, 1)
    bf_loads = table_loads(tf_hbm, bf, 2, 1)
    af_loads = table_loads(tf_hbm, af, 3, 0)

    loads[0].wait()
    for s in range(2):
        for part in range(2):
            win[s, 0, :, part * BLK:(part + 1) * BLK] = slab[s, part].astype(BF)

    pl.semaphore_wait(barrier, SPAN + 7)

    sends = []

    def start(copy):
        copy.start()
        sends.append(copy)

    for s in range(2):
        for k in range(2, SPAN + 1, 2):
            start(remote(
                win.at[s, 0], win.at[s, k], in_ss.at[s, k // 2], in_rs.at[s, k],
                lax.rem(t + tiles - k, tiles), x,
            ))

    def pass_on(s, m):
        k = 2 * m - 1 + 2 * c
        return remote(
            win.at[s, 2 * m], win.at[s, k], fw_ss.at[s, m], in_rs.at[s, k], pair + d, x)

    for s in range(2):
        @pl.when(c == 1)
        def _():
            pass_on(s, 0).start()

    loads[3].wait()
    loads[4].wait()
    for s in range(2):
        shape = (P_SIZE, P_SIZE + TH)
        shifted = lax.broadcasted_iota(jnp.int32, shape, 0) + off_ref[s]
        match = shifted == lax.broadcasted_iota(jnp.int32, shape, 1)
        sel[s] = jnp.where(match, 1.0, 0.0).astype(BF)
    loads[1].wait()
    for s in range(2):
        for r in range(2):
            ampb[s, r] = ampf[s, :, r * HALF:(r + 1) * HALF].astype(BF)

    def is_self(s, r):
        return jnp.logical_and(2 * s + c == x, c == r)

    def spread(src, dst, ss, rs, s, r):
        mine = is_self(s, r)

        @pl.when(mine)
        def _():
            pltpu.make_async_copy(src, dst.at[x], rs.at[x]).start()

        @pl.when(jnp.logical_not(mine))
        def _():
            remote(src, dst.at[x], ss.at[s, r], rs.at[x], pair + r, 2 * s + c).start()

    def spread_wait(src, dst, ss, rs, s, r):
        @pl.when(jnp.logical_not(is_self(s, r)))
        def _():
            remote(src, dst.at[x], ss.at[s, r], rs.at[x], pair + r, 2 * s + c).wait_send()

    def amp_of(s, r):
        return ampb.at[s, r], amp, am_ss, am_rs, s, r

    def h1_of(s, r):
        return h1.at[s, :, pl.ds(r * HALF, HALF), :], hr, h1_ss, h1_rs, s, r

    def o2_of(s, r):
        return o2p.at[s, :, pl.ds(r * HALF, HALF), :], o2r, o2_ss, o2_rs, s, r

    for s in range(2):
        for r in range(2):
            spread(*amp_of(s, r))

    table_ready(aq, aq_loads, 0)
    table_ready(bq, bq_loads, 1)
    table_ready(bf, bf_loads, 1)
    table_ready(af, af_loads, 0)

    def receive(dst, rs):
        pltpu.make_async_copy(dst, dst, rs).wait()

    def window(s):
        for m in range(1, 5):
            receive(win.at[s, 2 * m], in_rs.at[s, 2 * m])

            @pl.when(jnp.logical_or(c == 0, m < 4))
            def _():
                pass_on(s, m).start()
        for k in range(1, SPAN + 1, 2):
            receive(win.at[s, k], in_rs.at[s, k])
        return jnp.concatenate([win[s, k] for k in range(SPAN + 1)], axis=0)

    def dot(left, right):
        return jnp.dot(left, right, preferred_element_type=F32)

    loads[2].wait()
    wide = window(0)
    psi = []
    for s in range(2):
        patch = dot(sel[s], wide)
        pr, pi = probe[0].astype(F32), probe[1].astype(F32)
        fr, fi = patch[:, :BLK], patch[:, BLK:]
        psi.append(jnp.concatenate([
            (pr * fr - pi * fi).astype(BF), (pr * fi + pi * fr).astype(BF)], axis=0))
    psi = jnp.concatenate(psi, axis=1)
    for r in range(2):
        for part in range(2):
            at = part * P_SIZE + r * HALF
            half1 = dot(aq[at:at + HALF, :], psi).astype(BF)
            for s in range(2):
                h1[s, part, r * HALF:(r + 1) * HALF, :] = half1[:, s * BLK:(s + 1) * BLK]
        for s in range(2):
            spread(*h1_of(s, r))

    for s in range(2):
        for b, k in enumerate((1, 3, 5, 7, 2, 4, 6, 8, 0)):
            shape = (TH, P_SIZE)
            shifted = lax.broadcasted_iota(jnp.int32, shape, 1) + off_ref[s]
            match = shifted == lax.broadcasted_iota(jnp.int32, shape, 0) + k * TH
            alive = jnp.broadcast_to(cnt_ref[0], shape) > s
            put[b * TH:(b + 1) * TH, s * P_SIZE:(s + 1) * P_SIZE] = jnp.where(
                jnp.logical_and(match, alive), 1.0, 0.0).astype(BF)
    wide = window(1)
    for s in range(2):
        patch = dot(sel[s], wide).astype(BF)
        for part in range(2):
            o2p[s, part] = patch[:, part * BLK:(part + 1) * BLK]
        for r in range(2):
            spread(*o2_of(s, r))

    for n in range(4):
        receive(hr.at[n], h1_rs.at[n])
    left = jnp.concatenate([hr[n, part] for part in range(2) for n in range(4)], axis=1)
    for part in range(2):
        for h in range(2):
            at = part * P_SIZE + h * HALF
            ps[part, h] = dot(left, bq[:, at:at + HALF]).astype(BF)
    for n in range(4):
        receive(o2r.at[n], o2_rs.at[n])

    def second(part, h):
        return jnp.concatenate([o2r[2 * h, part], o2r[2 * h + 1, part]], axis=1).astype(F32)

    for h in range(2):
        wr, wi = ps[0, h].astype(F32), ps[1, h].astype(F32)
        sr, si = second(0, h), second(1, h)
        ew[:, h * HALF:(h + 1) * HALF] = (wr * sr - wi * si).astype(BF)
        ew[:, P_SIZE + h * HALF:P_SIZE + (h + 1) * HALF] = (wr * si + wi * sr).astype(BF)

    for part in range(2):
        at = pl.multiple_of(part * P_SIZE + d * HALF, HALF)
        gs[part] = dot(ew[...], bf[:, pl.ds(at, HALF)]).astype(BF)
    ex1 = remote(gs, x1.at[c], e1_ss, e1_rs, pair + d, x)
    ex1.start()
    for part in range(2):
        at = pl.multiple_of(part * P_SIZE + c * HALF, HALF)
        x1[c, part] = dot(ew[...], bf[:, pl.ds(at, HALF)]).astype(BF)
    for n in range(4):
        receive(amp.at[n], am_rs.at[n])
    receive(x1.at[d], e1_rs)

    right = jnp.concatenate([x1[r, part] for part in range(2) for r in range(2)], axis=0)
    for r in range(2):
        fr = dot(af[r * HALF:(r + 1) * HALF, :], right)
        fi = dot(af[P_SIZE + r * HALF:P_SIZE + (r + 1) * HALF, :], right)
        measured = jnp.concatenate([amp[2 * r], amp[2 * r + 1]], axis=0).astype(F32)
        keeping = 1.0 - measured / jnp.sqrt(fr * fr + fi * fi + smooth)
        ch[r * HALF:(r + 1) * HALF, :] = (fr * keeping).astype(BF)
        ch[P_SIZE + r * HALF:P_SIZE + (r + 1) * HALF, :] = (fi * keeping).astype(BF)

    for part in range(2):
        at = pl.multiple_of(part * P_SIZE + d * HALF, HALF)
        ks[part] = dot(bf[pl.ds(at, HALF), :], ch[...]).astype(BF)
    ex2 = remote(ks, y.at[c], e2_ss, e2_rs, pair + d, x)
    ex2.start()
    for part in range(2):
        at = pl.multiple_of(part * P_SIZE + c * HALF, HALF)
        y[c, part] = dot(bf[pl.ds(at, HALF), :], ch[...]).astype(BF)
    receive(y.at[d], e2_rs)

    left = jnp.concatenate([y[h, part] for part in range(2) for h in range(2)], axis=1)
    for h in range(2):
        er = dot(left, af[:, h * HALF:(h + 1) * HALF])
        ei = dot(left, af[:, P_SIZE + h * HALF:P_SIZE + (h + 1) * HALF])
        wr, wi = ps[0, h].astype(F32), ps[1, h].astype(F32)
        sr, si = second(0, h), second(1, h)
        tr, ti = (wr * er + wi * ei).astype(BF), (wr * ei - wi * er).astype(BF)
        for n in range(2):
            t2s[2 * h + n, 0] = tr[:, n * BLK:(n + 1) * BLK]
            t2s[2 * h + n, 1] = ti[:, n * BLK:(n + 1) * BLK]
        gw[:, h * HALF:(h + 1) * HALF] = (sr * er + si * ei).astype(BF)
        gw[:, P_SIZE + h * HALF:P_SIZE + (h + 1) * HALF] = (sr * ei - si * er).astype(BF)

    def is_home(n):
        return jnp.logical_and(home == t, x == n)

    def give(src, dst, ss, rs, n):
        where = dst.at[slot, :, pl.ds(pl.multiple_of(c * HALF, HALF), HALF), :]

        @pl.when(is_home(n))
        def _():
            pltpu.make_async_copy(src.at[n], where, rs.at[slot, c]).start()

        @pl.when(jnp.logical_not(is_home(n)))
        def _():
            remote(src.at[n], where, ss.at[n], rs.at[slot, c], home, n).start()

    def give_wait(src, dst, ss, rs, n):
        where = dst.at[slot, :, pl.ds(pl.multiple_of(c * HALF, HALF), HALF), :]

        @pl.when(jnp.logical_not(is_home(n)))
        def _():
            remote(src.at[n], where, ss.at[n], rs.at[slot, c], home, n).wait_send()

    for h in range(2):
        for part in range(2):
            at = part * P_SIZE + h * HALF
            back2 = dot(gw[...], aq[:, at:at + HALF]).astype(BF)
            for n in range(2):
                b2s[2 * h + n, part] = back2[:, n * BLK:(n + 1) * BLK]
        for n in range(2):
            give(b2s, b2r, b2_ss, b2_rs, 2 * h + n)
    for n in range(4):
        give(t2s, t2r, t2_ss, t2_rs, n)

    for s in range(2):
        for r in range(2):
            receive(b2r.at[s, :, pl.ds(r * HALF, HALF), :], b2_rs.at[s, r])
    right = jnp.concatenate([
        jnp.concatenate([b2r[0, part], b2r[1, part]], axis=1) for part in range(2)], axis=0)
    for r in range(2):
        nr = dot(bq[r * HALF:(r + 1) * HALF, :], right)
        ni = dot(bq[P_SIZE + r * HALF:P_SIZE + (r + 1) * HALF, :], right)
        pr = probe[0, r * HALF:(r + 1) * HALF, :].astype(F32)
        pi = probe[1, r * HALF:(r + 1) * HALF, :].astype(F32)
        for s in range(2):
            sr, si = nr[:, s * BLK:(s + 1) * BLK], ni[:, s * BLK:(s + 1) * BLK]
            rows = slice(s * P_SIZE + r * HALF, s * P_SIZE + (r + 1) * HALF)
            tp[rows, :BLK] = (pr * sr + pi * si).astype(BF)
            tp[rows, BLK:] = (pr * si - pi * sr).astype(BF)

    def collect(which, terms):
        total = dot(put[:HALF, :], terms)
        for m in range(4):
            odd[which, m] = total[m * TH:(m + 1) * TH].astype(BF)
            start(remote(
                odd.at[which, m], got.at[which, m], od_ss.at[which, m], od_rs.at[which, m],
                pair + d, x))
        total = dot(put[HALF:, :], terms)
        for m in range(1, 5):
            even[which, m] = total[(m - 1) * TH:m * TH]
        even[which, 0] = total[HALF:]

    def hand_on(which):
        for m in range(4):
            receive(got.at[which, m], od_rs.at[which, m])
            even[which, m + d] += got[which, m].astype(F32)
        for m in range(1, 5):
            outs[which, m] = even[which, m].astype(BF)
            start(remote(
                outs.at[which, m], oin.at[which, m], out_ss.at[which, m],
                out_rs.at[which, m], lax.rem(t + 2 * m, tiles), x))

    collect(0, tp[...])
    hand_on(0)
    for s in range(2):
        for r in range(2):
            receive(t2r.at[s, :, pl.ds(r * HALF, HALF), :], t2_rs.at[s, r])
    terms = jnp.concatenate([
        jnp.concatenate([t2r[s, part] for part in range(2)], axis=1) for s in range(2)], axis=0)
    collect(1, terms)
    hand_on(1)

    for which in range(2):
        total = even[which, 0]
        for m in range(1, 5):
            receive(oin.at[which, m], out_rs.at[which, m])
            total = total + oin[which, m].astype(F32)
        for part in range(2):
            out_ref[which, part] = total[:, part * BLK:(part + 1) * BLK]

    for copy in sends:
        copy.wait_send()
    for s in range(2):
        for m in range(5):
            @pl.when(jnp.logical_and(m < 4, c == 1) if m == 0 else jnp.logical_or(c == 0, m < 4))
            def _():
                pass_on(s, m).wait_send()
    ex1.wait_send()
    ex2.wait_send()
    for s in range(2):
        for r in range(2):
            spread_wait(*amp_of(s, r))
            spread_wait(*h1_of(s, r))
            spread_wait(*o2_of(s, r))
    for n in range(4):
        give_wait(b2s, b2r, b2_ss, b2_rs, n)
        give_wait(t2s, t2r, t2_ss, t2_rs, n)


def shards(tiles, far, near, object_slab, probe_wave, amplitudes, row_offsets, position_counts):
    dma = pltpu.SemaphoreType.DMA
    vmem = pltpu.VMEM
    n2 = 2 * P_SIZE
    scratch = [
        pltpu.SMEM((2,), jnp.int32), pltpu.SMEM((1,), jnp.int32),
        vmem((2, 2, TH, BLK), F32),
        vmem((2, P_SIZE, BLK), BF),
        vmem((2, BLK, P_SIZE), F32),
        vmem((n2, n2), BF), vmem((n2, n2), BF), vmem((n2, n2), BF), vmem((n2, n2), BF),
        vmem((2, SPAN + 1, TH, HALF), BF),
        vmem((2, P_SIZE, P_SIZE + TH), BF),
        vmem((P_SIZE + TH, n2), BF),
        vmem((2, 2, P_SIZE, BLK), BF),
        vmem((2, 2, P_SIZE, BLK), BF),
        vmem((2, 2, BLK, HALF), BF),
        vmem((4, 2, HALF, BLK), BF),
        vmem((4, 2, HALF, BLK), BF),
        vmem((4, BLK, HALF), BF),
        vmem((2, 2, HALF, HALF), BF),
        vmem((HALF, n2), BF),
        vmem((2, HALF, HALF), BF),
        vmem((2, 2, HALF, HALF), BF),
        vmem((n2, HALF), BF),
        vmem((2, HALF, HALF), BF),
        vmem((2, 2, HALF, HALF), BF),
        vmem((4, 2, HALF, BLK), BF),
        vmem((HALF, n2), BF),
        vmem((4, 2, HALF, BLK), BF),
        vmem((2, 2, P_SIZE, BLK), BF),
        vmem((2, 2, P_SIZE, BLK), BF),
        vmem((n2, HALF), BF),
        vmem((2, 4, TH, HALF), BF),
        vmem((2, 4, TH, HALF), BF),
        vmem((2, 5, TH, HALF), F32),
        vmem((2, 5, TH, HALF), BF),
        vmem((2, 5, TH, HALF), BF),
        dma((5,)), dma((4, 3)),
        dma((2, 5)), dma((2, SPAN + 1)), dma((2, 5)),
        dma((2, 2)), dma((4,)), dma((2, 2)), dma((4,)), dma((2, 2)), dma((4,)),
        dma, dma, dma, dma,
        dma((4,)), dma((2, 2)), dma((4,)), dma((2, 2)),
        dma((2, 4)), dma((2, 4)), dma((2, 5)), dma((2, 5)),
    ]
    any_spec = pl.BlockSpec(memory_space=pl.ANY)
    return pl.pallas_call(
        functools.partial(body, tiles),
        out_shape=jax.ShapeDtypeStruct(object_slab.shape, F32),
        in_specs=[any_spec] * 7,
        out_specs=pl.BlockSpec(memory_space=pltpu.VMEM),
        scratch_shapes=scratch,
        compiler_params=pltpu.CompilerParams(
            collective_id=0, has_side_effects=True, vmem_limit_bytes=67_000_000
        ),
        name="object_gradient",
    )(row_offsets, position_counts, object_slab, probe_wave, amplitudes, near, far)


def solution(mesh):
    in_specs = (
        P(None, None, "tile", "scan"),
        P(None, None, "scan"),
        P("tile", "scan", None),
        P("tile"),
        P("tile"),
    )
    out_specs = P(None, None, "tile", "scan")
    far, near = tables()
    run = functools.partial(shards, mesh.shape["tile"], far, near)
    return jax.shard_map(run, mesh=mesh, in_specs=in_specs, out_specs=out_specs, check_vma=False)
```

```python
import functools
import math

import jax
import jax.numpy as jnp
import numpy as np
from jax import lax
from jax.experimental import pallas as pl
from jax.experimental.pallas import tpu as pltpu
from jax.sharding import PartitionSpec as P

P_SIZE = 512
HALF = 256
BLK = 128
TH = 64
SPAN = P_SIZE // TH

fresnel = 0.5
smooth = 1.0
MESH = pl.DeviceIdType.MESH
BF = jnp.bfloat16
F32 = jnp.float32


def tables():
    index = np.arange(P_SIZE)
    angles = 2.0 * np.pi / P_SIZE * (index[:, None] * index[None, :] % P_SIZE)
    wave = np.exp(1j * angles)
    far = np.conj(wave) / math.sqrt(P_SIZE)
    centred = np.where(index < P_SIZE // 2, index, index - P_SIZE).astype(np.float64)
    kernel = np.exp(-1j * np.pi * fresnel / P_SIZE * centred * centred)
    near = (wave * kernel[None, :]) @ np.conj(wave).T / P_SIZE

    def planes(table):
        both = np.stack([table.real, table.imag])
        return both.astype(np.float32).astype(BF)

    return planes(far), planes(near)


def body(
    tiles,
    off_hbm, cnt_hbm, slab_hbm, probe_hbm, amp_hbm, tq_hbm, tf_hbm,
    out_ref,
    off_ref, cnt_ref, slab, probe, ampf, aq, bq, af, bf,
    win, o2g, o2w, offb, sel, psel, put, h1, ampb, hr, o2r, amp,
    ps, ew, gs, x1, ch, ks, y, t2s, gw, b2s, b2r, t2r, tp, odd, got, even, outs, oin,
    loc_sem, tab_sem,
    in_ss, in_rs, fw_ss, og_ss, og_rs, up_ss, up_rs, of_ss, of_rs,
    h1_ss, h1_rs, o2_ss, o2_rs, am_ss, am_rs,
    e1_ss, e1_rs, e2_ss, e2_rs, b2_ss, b2_rs, t2_ss, t2_rs, od_ss, od_rs, out_ss, out_rs,
):
    t = lax.axis_index("tile")
    x = lax.axis_index("scan")
    c = lax.rem(t, 2)
    d = 1 - c
    pair = t - c
    home = pair + lax.rem(x, 2)
    slot = x // 2
    odd_home = lax.rem(x, 2)
    row = lax.rem(t // 2, 4)
    plane = t - lax.rem(t, 8)

    def remote(src, dst, ss, rs, tile, scan):
        return pltpu.make_async_remote_copy(
            src_ref=src, dst_ref=dst, send_sem=ss, recv_sem=rs,
            device_id={"tile": tile, "scan": scan}, device_id_type=MESH,
        )

    loads = [
        pltpu.make_async_copy(slab_hbm, slab, loc_sem.at[0]),
        pltpu.make_async_copy(amp_hbm, ampf, loc_sem.at[1]),
        pltpu.make_async_copy(probe_hbm, probe, loc_sem.at[2]),
        pltpu.make_async_copy(off_hbm, off_ref, loc_sem.at[3]),
        pltpu.make_async_copy(cnt_hbm, cnt_ref, loc_sem.at[4]),
    ]
    for load in loads:
        load.start()

    barrier = pltpu.get_barrier_semaphore()

    def greet(tile, scan):
        pl.semaphore_signal(
            barrier, inc=1, device_id={"tile": tile, "scan": scan}, device_id_type=MESH
        )

    for n in range(1, 8):
        greet(plane + lax.rem(t + n, 8), x)
    for k in range(2, SPAN + 1, 2):
        greet(lax.rem(t + k, tiles), x)
        greet(lax.rem(t + tiles - k, tiles), x)
    for step in range(1, 4):
        for core in range(2):
            greet(pair + core, lax.rem(x + step, 4))

    def table_loads(src, dst, which, column):
        copies = []
        for n, (up, left, plane) in enumerate([(0, 0, 0), (1 - column, column, 1), (1, 1, 0)]):
            where = dst.at[pl.ds(up * P_SIZE, P_SIZE), pl.ds(left * P_SIZE, P_SIZE)]
            copies.append(pltpu.make_async_copy(src.at[plane], where, tab_sem.at[which, n]))
        for copy in copies:
            copy.start()
        return copies

    def table_ready(dst, copies, column):
        for copy in copies:
            copy.wait()
        imag = dst[(1 - column) * P_SIZE:(2 - column) * P_SIZE, column * P_SIZE:(column + 1) * P_SIZE]
        dst[column * P_SIZE:(column + 1) * P_SIZE, (1 - column) * P_SIZE:(2 - column) * P_SIZE] = -imag

    aq_loads = table_loads(tq_hbm, aq, 0, 0)
    bq_loads = table_loads(tq_hbm, bq, 1, 1)
    bf_loads = table_loads(tf_hbm, bf, 2, 1)
    af_loads = table_loads(tf_hbm, af, 3, 0)

    loads[0].wait()
    for part in range(2):
        win[0, :, part * BLK:(part + 1) * BLK] = slab[0, part].astype(BF)
        o2g[0, x, :, part * BLK:(part + 1) * BLK] = slab[1, part].astype(BF)
    loads[3].wait()
    loads[4].wait()
    shape = (8, 3 * BLK)
    offset = jnp.broadcast_to(off_ref[slot], shape)
    alive = jnp.broadcast_to(cnt_ref[0], shape) > jnp.broadcast_to(slot, shape)
    offb[c] = jnp.where(alive, offset, -2 * P_SIZE).astype(F32)

    pl.semaphore_wait(barrier, SPAN + 13)

    sends = []

    def start(copy):
        copy.start()
        sends.append(copy)

    for k in range(2, SPAN + 1, 2):
        start(remote(
            win.at[0], win.at[k], in_ss.at[k // 2], in_rs.at[k], lax.rem(t + tiles - k, tiles), x))

    def pass_on(m):
        k = 2 * m - 1 + 2 * c
        return remote(win.at[2 * m], win.at[k], fw_ss.at[m], in_rs.at[k], pair + d, x)

    @pl.when(c == 1)
    def _():
        pass_on(0).start()

    for step in range(1, 4):
        start(remote(
            o2g.at[0, x], o2g.at[0, x], og_ss.at[step - 1], og_rs.at[x],
            t, lax.rem(x + step, 4)))
    start(remote(offb.at[c], offb.at[c], of_ss, of_rs, pair + d, x))

    for s in range(2):
        shape = (P_SIZE, P_SIZE + TH)
        shifted = lax.broadcasted_iota(jnp.int32, shape, 0) + off_ref[s]
        match = shifted == lax.broadcasted_iota(jnp.int32, shape, 1)
        sel[s] = jnp.where(match, 1.0, 0.0).astype(BF)
    loads[1].wait()
    for s in range(2):
        for r in range(2):
            ampb[s, r] = ampf[s, :, r * HALF:(r + 1) * HALF].astype(BF)

    def is_self(s, r):
        return jnp.logical_and(2 * s + c == x, c == r)

    def spread(src, dst, ss, rs, s, r):
        mine = is_self(s, r)

        @pl.when(mine)
        def _():
            pltpu.make_async_copy(src, dst.at[x], rs.at[x]).start()

        @pl.when(jnp.logical_not(mine))
        def _():
            remote(src, dst.at[x], ss.at[s, r], rs.at[x], pair + r, 2 * s + c).start()

    def spread_wait(src, dst, ss, rs, s, r):
        @pl.when(jnp.logical_not(is_self(s, r)))
        def _():
            remote(src, dst.at[x], ss.at[s, r], rs.at[x], pair + r, 2 * s + c).wait_send()

    def amp_of(s, r):
        return ampb.at[s, r], amp, am_ss, am_rs, s, r

    def h1_of(s, r):
        return h1.at[s, :, pl.ds(r * HALF, HALF), :], hr, h1_ss, h1_rs, s, r

    for s in range(2):
        for r in range(2):
            spread(*amp_of(s, r))

    table_ready(aq, aq_loads, 0)
    table_ready(bq, bq_loads, 1)
    table_ready(bf, bf_loads, 1)
    table_ready(af, af_loads, 0)

    def receive(dst, rs):
        pltpu.make_async_copy(dst, dst, rs).wait()

    def plane_send(m, r, go, local):
        place = 2 * m + c - odd_home - 4 * r
        wanted = jnp.logical_and(place >= 0, place <= 4)
        for source in range(2):
            if m in (0, 4):
                if source != m // 4:
                    continue
                tile, here = pair + r, wanted
            else:
                tile = plane + 2 * lax.rem(row - m + 4, 4) + r
                here = jnp.logical_and(wanted, (m <= row) if source == 0 else (m > row))

            def copy():
                return remote(
                    o2g.at[source], o2w.at[place], o2_ss.at[m, r], o2_rs.at[place], tile, x)

            def own():
                return pltpu.make_async_copy(o2g.at[source], o2w.at[place], o2_rs.at[place])

            if source in go:
                if m in (0, 4):
                    @pl.when(jnp.logical_and(here, c != r))
                    def _():
                        copy().start() if local else copy().wait_send()

                    if local:
                        @pl.when(jnp.logical_and(here, c == r))
                        def _():
                            own().start()
                else:
                    @pl.when(here)
                    def _():
                        copy().start() if local else copy().wait_send()

    for step in range(1, 4):
        other = lax.rem(x + step, 4)
        receive(o2g.at[0, other], og_rs.at[other])
    start(remote(o2g.at[0], o2g.at[1], up_ss, up_rs, lax.rem(t + tiles - 8, tiles), x))
    for m in range(4):
        for r in range(2):
            plane_send(m, r, (0,), True)

    def window():
        for m in range(1, 5):
            receive(win.at[2 * m], in_rs.at[2 * m])

            @pl.when(jnp.logical_or(c == 0, m < 4))
            def _():
                pass_on(m).start()
        for k in range(1, SPAN + 1, 2):
            receive(win.at[k], in_rs.at[k])
        return jnp.concatenate([win[k] for k in range(SPAN + 1)], axis=0)

    def dot(left, right):
        return jnp.dot(left, right, preferred_element_type=F32)

    loads[2].wait()
    wide = window()
    psi = []
    for s in range(2):
        patch = dot(sel[s], wide)
        pr, pi = probe[0].astype(F32), probe[1].astype(F32)
        fr, fi = patch[:, :BLK], patch[:, BLK:]
        psi.append(jnp.concatenate([
            (pr * fr - pi * fi).astype(BF), (pr * fi + pi * fr).astype(BF)], axis=0))
    psi = jnp.concatenate(psi, axis=1)
    for r in range(2):
        for part in range(2):
            at = part * P_SIZE + r * HALF
            half1 = dot(aq[at:at + HALF, :], psi).astype(BF)
            for s in range(2):
                h1[s, part, r * HALF:(r + 1) * HALF, :] = half1[:, s * BLK:(s + 1) * BLK]
        for s in range(2):
            spread(*h1_of(s, r))

    receive(o2g.at[1], up_rs)
    for m in range(1, 5):
        for r in range(2):
            plane_send(m, r, (1,), True)

    for s in range(2):
        for b, k in enumerate((1, 3, 5, 7, 2, 4, 6, 8, 0)):
            shape = (TH, P_SIZE)
            shifted = lax.broadcasted_iota(jnp.int32, shape, 1) + off_ref[s]
            match = shifted == lax.broadcasted_iota(jnp.int32, shape, 0) + k * TH
            alive = jnp.broadcast_to(cnt_ref[0], shape) > s
            put[b * TH:(b + 1) * TH, s * P_SIZE:(s + 1) * P_SIZE] = jnp.where(
                jnp.logical_and(match, alive), 1.0, 0.0).astype(BF)
    receive(offb.at[d], of_rs)
    shape = (HALF, HALF + TH)
    shifted = lax.broadcasted_iota(jnp.int32, shape, 0).astype(F32) + offb[odd_home][0:1, :HALF + TH]
    match = shifted == lax.broadcasted_iota(jnp.int32, shape, 1).astype(F32)
    psel[...] = jnp.where(match, 1.0, 0.0).astype(BF)

    for n in range(4):
        receive(hr.at[n], h1_rs.at[n])
    left = jnp.concatenate([hr[n, part] for part in range(2) for n in range(4)], axis=1)
    for part in range(2):
        for h in range(2):
            at = part * P_SIZE + h * HALF
            ps[part, h] = dot(left, bq[:, at:at + HALF]).astype(BF)
    for k in range(5):
        receive(o2w.at[k], o2_rs.at[k])
    for n in range(4):
        rows = jnp.concatenate([o2w[k, n] for k in range(5)], axis=0)
        o2r[n] = dot(psel[...], rows).astype(BF)

    def second(part, h):
        columns = slice(part * BLK, (part + 1) * BLK)
        return jnp.concatenate([o2r[2 * h, :, columns], o2r[2 * h + 1, :, columns]], axis=1).astype(F32)

    for h in range(2):
        wr, wi = ps[0, h].astype(F32), ps[1, h].astype(F32)
        sr, si = second(0, h), second(1, h)
        ew[:, h * HALF:(h + 1) * HALF] = (wr * sr - wi * si).astype(BF)
        ew[:, P_SIZE + h * HALF:P_SIZE + (h + 1) * HALF] = (wr * si + wi * sr).astype(BF)

    for part in range(2):
        at = pl.multiple_of(part * P_SIZE + d * HALF, HALF)
        gs[part] = dot(ew[...], bf[:, pl.ds(at, HALF)]).astype(BF)
    ex1 = remote(gs, x1.at[c], e1_ss, e1_rs, pair + d, x)
    ex1.start()
    for part in range(2):
        at = pl.multiple_of(part * P_SIZE + c * HALF, HALF)
        x1[c, part] = dot(ew[...], bf[:, pl.ds(at, HALF)]).astype(BF)
    for n in range(4):
        receive(amp.at[n], am_rs.at[n])
    receive(x1.at[d], e1_rs)

    right = jnp.concatenate([x1[r, part] for part in range(2) for r in range(2)], axis=0)
    for r in range(2):
        fr = dot(af[r * HALF:(r + 1) * HALF, :], right)
        fi = dot(af[P_SIZE + r * HALF:P_SIZE + (r + 1) * HALF, :], right)
        measured = jnp.concatenate([amp[2 * r], amp[2 * r + 1]], axis=0).astype(F32)
        keeping = 1.0 - measured / jnp.sqrt(fr * fr + fi * fi + smooth)
        ch[r * HALF:(r + 1) * HALF, :] = (fr * keeping).astype(BF)
        ch[P_SIZE + r * HALF:P_SIZE + (r + 1) * HALF, :] = (fi * keeping).astype(BF)

    for part in range(2):
        at = pl.multiple_of(part * P_SIZE + d * HALF, HALF)
        ks[part] = dot(bf[pl.ds(at, HALF), :], ch[...]).astype(BF)
    ex2 = remote(ks, y.at[c], e2_ss, e2_rs, pair + d, x)
    ex2.start()
    for part in range(2):
        at = pl.multiple_of(part * P_SIZE + c * HALF, HALF)
        y[c, part] = dot(bf[pl.ds(at, HALF), :], ch[...]).astype(BF)
    receive(y.at[d], e2_rs)

    left = jnp.concatenate([y[h, part] for part in range(2) for h in range(2)], axis=1)
    for h in range(2):
        er = dot(left, af[:, h * HALF:(h + 1) * HALF])
        ei = dot(left, af[:, P_SIZE + h * HALF:P_SIZE + (h + 1) * HALF])
        wr, wi = ps[0, h].astype(F32), ps[1, h].astype(F32)
        sr, si = second(0, h), second(1, h)
        tr, ti = (wr * er + wi * ei).astype(BF), (wr * ei - wi * er).astype(BF)
        for n in range(2):
            t2s[2 * h + n, 0] = tr[:, n * BLK:(n + 1) * BLK]
            t2s[2 * h + n, 1] = ti[:, n * BLK:(n + 1) * BLK]
        gw[:, h * HALF:(h + 1) * HALF] = (sr * er + si * ei).astype(BF)
        gw[:, P_SIZE + h * HALF:P_SIZE + (h + 1) * HALF] = (sr * ei - si * er).astype(BF)

    def is_home(n):
        return jnp.logical_and(home == t, x == n)

    def give(src, dst, ss, rs, n):
        where = dst.at[slot, :, pl.ds(pl.multiple_of(c * HALF, HALF), HALF), :]

        @pl.when(is_home(n))
        def _():
            pltpu.make_async_copy(src.at[n], where, rs.at[slot, c]).start()

        @pl.when(jnp.logical_not(is_home(n)))
        def _():
            remote(src.at[n], where, ss.at[n], rs.at[slot, c], home, n).start()

    def give_wait(src, dst, ss, rs, n):
        where = dst.at[slot, :, pl.ds(pl.multiple_of(c * HALF, HALF), HALF), :]

        @pl.when(jnp.logical_not(is_home(n)))
        def _():
            remote(src.at[n], where, ss.at[n], rs.at[slot, c], home, n).wait_send()

    for h in range(2):
        for part in range(2):
            at = part * P_SIZE + h * HALF
            back2 = dot(gw[...], aq[:, at:at + HALF]).astype(BF)
            for n in range(2):
                b2s[2 * h + n, part] = back2[:, n * BLK:(n + 1) * BLK]
        for n in range(2):
            give(b2s, b2r, b2_ss, b2_rs, 2 * h + n)
    for n in range(4):
        give(t2s, t2r, t2_ss, t2_rs, n)

    for s in range(2):
        for r in range(2):
            receive(b2r.at[s, :, pl.ds(r * HALF, HALF), :], b2_rs.at[s, r])
    right = jnp.concatenate([
        jnp.concatenate([b2r[0, part], b2r[1, part]], axis=1) for part in range(2)], axis=0)
    for r in range(2):
        nr = dot(bq[r * HALF:(r + 1) * HALF, :], right)
        ni = dot(bq[P_SIZE + r * HALF:P_SIZE + (r + 1) * HALF, :], right)
        pr = probe[0, r * HALF:(r + 1) * HALF, :].astype(F32)
        pi = probe[1, r * HALF:(r + 1) * HALF, :].astype(F32)
        for s in range(2):
            sr, si = nr[:, s * BLK:(s + 1) * BLK], ni[:, s * BLK:(s + 1) * BLK]
            rows = slice(s * P_SIZE + r * HALF, s * P_SIZE + (r + 1) * HALF)
            tp[rows, :BLK] = (pr * sr + pi * si).astype(BF)
            tp[rows, BLK:] = (pr * si - pi * sr).astype(BF)

    def collect(which, terms):
        total = dot(put[:HALF, :], terms)
        for m in range(4):
            odd[which, m] = total[m * TH:(m + 1) * TH].astype(BF)
            start(remote(
                odd.at[which, m], got.at[which, m], od_ss.at[which, m], od_rs.at[which, m],
                pair + d, x))
        total = dot(put[HALF:, :], terms)
        for m in range(1, 5):
            even[which, m] = total[(m - 1) * TH:m * TH]
        even[which, 0] = total[HALF:]

    def hand_on(which):
        for m in range(4):
            receive(got.at[which, m], od_rs.at[which, m])
            even[which, m + d] += got[which, m].astype(F32)
        for m in range(1, 5):
            outs[which, m] = even[which, m].astype(BF)
            start(remote(
                outs.at[which, m], oin.at[which, m], out_ss.at[which, m],
                out_rs.at[which, m], lax.rem(t + 2 * m, tiles), x))

    collect(0, tp[...])
    hand_on(0)
    for s in range(2):
        for r in range(2):
            receive(t2r.at[s, :, pl.ds(r * HALF, HALF), :], t2_rs.at[s, r])
    terms = jnp.concatenate([
        jnp.concatenate([t2r[s, part] for part in range(2)], axis=1) for s in range(2)], axis=0)
    collect(1, terms)
    hand_on(1)

    for which in range(2):
        total = even[which, 0]
        for m in range(1, 5):
            receive(oin.at[which, m], out_rs.at[which, m])
            total = total + oin[which, m].astype(F32)
        for part in range(2):
            out_ref[which, part] = total[:, part * BLK:(part + 1) * BLK]

    for copy in sends:
        copy.wait_send()
    for m in range(5):
        @pl.when((c == 1) if m == 0 else jnp.logical_or(c == 0, m < 4))
        def _():
            pass_on(m).wait_send()
        for r in range(2):
            plane_send(m, r, (0, 1), False)
    ex1.wait_send()
    ex2.wait_send()
    for s in range(2):
        for r in range(2):
            spread_wait(*amp_of(s, r))
            spread_wait(*h1_of(s, r))
    for n in range(4):
        give_wait(b2s, b2r, b2_ss, b2_rs, n)
        give_wait(t2s, t2r, t2_ss, t2_rs, n)


def shards(tiles, far, near, object_slab, probe_wave, amplitudes, row_offsets, position_counts):
    dma = pltpu.SemaphoreType.DMA
    vmem = pltpu.VMEM
    n2 = 2 * P_SIZE
    scratch = [
        pltpu.SMEM((2,), jnp.int32), pltpu.SMEM((1,), jnp.int32),
        vmem((2, 2, TH, BLK), F32),
        vmem((2, P_SIZE, BLK), BF),
        vmem((2, BLK, P_SIZE), F32),
        vmem((n2, n2), BF), vmem((n2, n2), BF), vmem((n2, n2), BF), vmem((n2, n2), BF),
        vmem((SPAN + 1, TH, HALF), BF),
        vmem((2, 4, TH, HALF), BF),
        vmem((5, 4, TH, HALF), BF),
        vmem((2, 8, 3 * BLK), F32),
        vmem((2, P_SIZE, P_SIZE + TH), BF),
        vmem((HALF, HALF + TH), BF),
        vmem((P_SIZE + TH, n2), BF),
        vmem((2, 2, P_SIZE, BLK), BF),
        vmem((2, 2, BLK, HALF), BF),
        vmem((4, 2, HALF, BLK), BF),
        vmem((4, HALF, HALF), BF),
        vmem((4, BLK, HALF), BF),
        vmem((2, 2, HALF, HALF), BF),
        vmem((HALF, n2), BF),
        vmem((2, HALF, HALF), BF),
        vmem((2, 2, HALF, HALF), BF),
        vmem((n2, HALF), BF),
        vmem((2, HALF, HALF), BF),
        vmem((2, 2, HALF, HALF), BF),
        vmem((4, 2, HALF, BLK), BF),
        vmem((HALF, n2), BF),
        vmem((4, 2, HALF, BLK), BF),
        vmem((2, 2, P_SIZE, BLK), BF),
        vmem((2, 2, P_SIZE, BLK), BF),
        vmem((n2, HALF), BF),
        vmem((2, 4, TH, HALF), BF),
        vmem((2, 4, TH, HALF), BF),
        vmem((2, 5, TH, HALF), F32),
        vmem((2, 5, TH, HALF), BF),
        vmem((2, 5, TH, HALF), BF),
        dma((5,)), dma((4, 3)),
        dma((5,)), dma((SPAN + 1,)), dma((5,)), dma((3,)), dma((4,)), dma, dma, dma, dma,
        dma((2, 2)), dma((4,)), dma((5, 2)), dma((5,)), dma((2, 2)), dma((4,)),
        dma, dma, dma, dma,
        dma((4,)), dma((2, 2)), dma((4,)), dma((2, 2)),
        dma((2, 4)), dma((2, 4)), dma((2, 5)), dma((2, 5)),
    ]
    any_spec = pl.BlockSpec(memory_space=pl.ANY)
    return pl.pallas_call(
        functools.partial(body, tiles),
        out_shape=jax.ShapeDtypeStruct(object_slab.shape, F32),
        in_specs=[any_spec] * 7,
        out_specs=pl.BlockSpec(memory_space=pltpu.VMEM),
        scratch_shapes=scratch,
        compiler_params=pltpu.CompilerParams(
            collective_id=0, has_side_effects=True, vmem_limit_bytes=67_000_000
        ),
        name="object_gradient",
    )(row_offsets, position_counts, object_slab, probe_wave, amplitudes, near, far)


def solution(mesh):
    in_specs = (
        P(None, None, "tile", "scan"),
        P(None, None, "scan"),
        P("tile", "scan", None),
        P("tile"),
        P("tile"),
    )
    out_specs = P(None, None, "tile", "scan")
    far, near = tables()
    run = functools.partial(shards, mesh.shape["tile"], far, near)
    return jax.shard_map(run, mesh=mesh, in_specs=in_specs, out_specs=out_specs, check_vma=False)
```

```python
import functools
import math

import jax
import jax.numpy as jnp
import numpy as np
from jax import lax
from jax.experimental import pallas as pl
from jax.experimental.pallas import tpu as pltpu
from jax.sharding import PartitionSpec as P

P_SIZE = 512
HALF = 256
BLK = 128
TH = 64
SPAN = P_SIZE // TH

fresnel = 0.5
smooth = 1.0
MESH = pl.DeviceIdType.MESH
BF = jnp.bfloat16
F32 = jnp.float32


def tables():
    index = np.arange(P_SIZE)
    angles = 2.0 * np.pi / P_SIZE * (index[:, None] * index[None, :] % P_SIZE)
    wave = np.exp(1j * angles)
    far = np.conj(wave) / math.sqrt(P_SIZE)
    centred = np.where(index < P_SIZE // 2, index, index - P_SIZE).astype(np.float64)
    kernel = np.exp(-1j * np.pi * fresnel / P_SIZE * centred * centred)
    near = (wave * kernel[None, :]) @ np.conj(wave).T / P_SIZE

    def planes(table):
        both = np.stack([table.real, table.imag])
        return both.astype(np.float32).astype(BF)

    return planes(far), planes(near)


def body(
    tiles,
    off_hbm, cnt_hbm, slab_hbm, probe_hbm, amp_hbm, tq_hbm, tf_hbm,
    out_ref,
    off_ref, cnt_ref, slab, probe, ampf, aq, bq, af, bf,
    win, o2g, o2w, offb, sel, psel, put, h1, ampb, hr, o2r, amp,
    ps, ew, gs, x1, ch, ks, y, t2s, gw, b2s, b2r, tp, odd, got, even, outs, oin,
    pput, t2o, rin, acc, uo, ui, xo, xi,
    loc_sem, tab_sem,
    in_ss, in_rs, fw_ss, og_ss, og_rs, up_ss, up_rs, of_ss, of_rs,
    h1_ss, h1_rs, o2_ss, o2_rs, am_ss, am_rs,
    e1_ss, e1_rs, e2_ss, e2_rs, b2_ss, b2_rs, rt_ss, rt_rs, uu_ss, uu_rs, xs_ss, xs_rs, od_ss, od_rs, out_ss, out_rs,
):
    t = lax.axis_index("tile")
    x = lax.axis_index("scan")
    c = lax.rem(t, 2)
    d = 1 - c
    pair = t - c
    home = pair + lax.rem(x, 2)
    slot = x // 2
    odd_home = lax.rem(x, 2)
    row = lax.rem(t // 2, 4)
    plane = t - lax.rem(t, 8)

    def remote(src, dst, ss, rs, tile, scan):
        return pltpu.make_async_remote_copy(
            src_ref=src, dst_ref=dst, send_sem=ss, recv_sem=rs,
            device_id={"tile": tile, "scan": scan}, device_id_type=MESH,
        )

    loads = [
        pltpu.make_async_copy(slab_hbm, slab, loc_sem.at[0]),
        pltpu.make_async_copy(amp_hbm, ampf, loc_sem.at[1]),
        pltpu.make_async_copy(probe_hbm, probe, loc_sem.at[2]),
        pltpu.make_async_copy(off_hbm, off_ref, loc_sem.at[3]),
        pltpu.make_async_copy(cnt_hbm, cnt_ref, loc_sem.at[4]),
    ]
    for load in loads:
        load.start()

    barrier = pltpu.get_barrier_semaphore()

    def greet(tile, scan):
        pl.semaphore_signal(
            barrier, inc=1, device_id={"tile": tile, "scan": scan}, device_id_type=MESH
        )

    for n in range(1, 8):
        greet(plane + lax.rem(t + n, 8), x)
    def below(k):
        return t - k >= 0

    def above(k):
        return t + k < tiles

    for k in range(2, SPAN + 1, 2):
        @pl.when(above(k))
        def _():
            greet(t + k, x)

        @pl.when(below(k))
        def _():
            greet(t - k, x)
    for step in range(1, 4):
        for core in range(2):
            greet(pair + core, lax.rem(x + step, 4))

    def table_loads(src, dst, which, column):
        copies = []
        for n, (up, left, plane) in enumerate([(0, 0, 0), (1 - column, column, 1), (1, 1, 0)]):
            where = dst.at[pl.ds(up * P_SIZE, P_SIZE), pl.ds(left * P_SIZE, P_SIZE)]
            copies.append(pltpu.make_async_copy(src.at[plane], where, tab_sem.at[which, n]))
        for copy in copies:
            copy.start()
        return copies

    def table_ready(dst, copies, column):
        for copy in copies:
            copy.wait()
        imag = dst[(1 - column) * P_SIZE:(2 - column) * P_SIZE, column * P_SIZE:(column + 1) * P_SIZE]
        dst[column * P_SIZE:(column + 1) * P_SIZE, (1 - column) * P_SIZE:(2 - column) * P_SIZE] = -imag

    aq_loads = table_loads(tq_hbm, aq, 0, 0)
    bq_loads = table_loads(tq_hbm, bq, 1, 1)
    bf_loads = table_loads(tf_hbm, bf, 2, 1)
    af_loads = table_loads(tf_hbm, af, 3, 0)

    loads[0].wait()
    for part in range(2):
        win[0, :, part * BLK:(part + 1) * BLK] = slab[0, part].astype(BF)
        o2g[0, x, :, part * BLK:(part + 1) * BLK] = slab[1, part].astype(BF)
    loads[3].wait()
    loads[4].wait()
    shape = (8, 3 * BLK)
    offset = jnp.broadcast_to(off_ref[slot], shape)
    alive = jnp.broadcast_to(cnt_ref[0], shape) > jnp.broadcast_to(slot, shape)
    offb[c] = jnp.where(alive, offset, -2 * P_SIZE).astype(F32)

    for m in range(1, 5):
        @pl.when(jnp.logical_not(above(2 * m)))
        def _():
            win[2 * m] = jnp.zeros((TH, HALF), BF)

        @pl.when(jnp.logical_not(below(2 * m)))
        def _():
            oin[0, m] = jnp.zeros((TH, HALF), BF)

    @pl.when(jnp.logical_not(above(8)))
    def _():
        o2g[1] = jnp.zeros((4, TH, HALF), BF)

    @pl.when(jnp.logical_not(below(8)))
    def _():
        ui[...] = jnp.zeros((4, TH, HALF), BF)

    pl.semaphore_wait(
        barrier, 13 + jnp.minimum(4, (tiles - 1 - t) // 2) + jnp.minimum(4, t // 2))

    sends = []

    def start(copy, here=None):
        sends.append((copy, here))
        if here is None:
            copy.start()
        else:
            pl.when(here)(copy.start)

    def receive(dst, rs, here=None):
        copy = pltpu.make_async_copy(dst, dst, rs)
        if here is None:
            copy.wait()
        else:
            pl.when(here)(copy.wait)

    for k in range(2, SPAN + 1, 2):
        start(remote(
            win.at[0], win.at[k], in_ss.at[k // 2], in_rs.at[k], t - k, x), below(k))

    def pass_on(m):
        k = 2 * m - 1 + 2 * c
        return remote(win.at[2 * m], win.at[k], fw_ss.at[m], in_rs.at[k], pair + d, x)

    @pl.when(c == 1)
    def _():
        pass_on(0).start()

    for step in range(1, 4):
        start(remote(
            o2g.at[0, x], o2g.at[0, x], og_ss.at[step - 1], og_rs.at[x],
            t, lax.rem(x + step, 4)))
    start(remote(offb.at[c], offb.at[c], of_ss, of_rs, pair + d, x))

    for s in range(2):
        shape = (P_SIZE, P_SIZE + TH)
        shifted = lax.broadcasted_iota(jnp.int32, shape, 0) + off_ref[s]
        match = shifted == lax.broadcasted_iota(jnp.int32, shape, 1)
        sel[s] = jnp.where(match, 1.0, 0.0).astype(BF)
    loads[1].wait()
    for s in range(2):
        for r in range(2):
            ampb[s, r] = ampf[s, :, r * HALF:(r + 1) * HALF].astype(BF)

    def is_self(s, r):
        return jnp.logical_and(2 * s + c == x, c == r)

    def spread(src, dst, ss, rs, s, r):
        mine = is_self(s, r)

        @pl.when(mine)
        def _():
            pltpu.make_async_copy(src, dst.at[x], rs.at[x]).start()

        @pl.when(jnp.logical_not(mine))
        def _():
            remote(src, dst.at[x], ss.at[s, r], rs.at[x], pair + r, 2 * s + c).start()

    def spread_wait(src, dst, ss, rs, s, r):
        @pl.when(jnp.logical_not(is_self(s, r)))
        def _():
            remote(src, dst.at[x], ss.at[s, r], rs.at[x], pair + r, 2 * s + c).wait_send()

    def amp_of(s, r):
        return ampb.at[s, r], amp, am_ss, am_rs, s, r

    def h1_of(s, r):
        return h1.at[s, :, pl.ds(r * HALF, HALF), :], hr, h1_ss, h1_rs, s, r

    for s in range(2):
        for r in range(2):
            spread(*amp_of(s, r))

    table_ready(aq, aq_loads, 0)
    table_ready(bq, bq_loads, 1)
    table_ready(bf, bf_loads, 1)
    table_ready(af, af_loads, 0)

    def plane_send(m, r, go, local):
        place = 2 * m + c - odd_home - 4 * r
        wanted = jnp.logical_and(place >= 0, place <= 4)
        for source in range(2):
            if m in (0, 4):
                if source != m // 4:
                    continue
                tile, here = pair + r, wanted
            else:
                tile = plane + 2 * lax.rem(row - m + 4, 4) + r
                here = jnp.logical_and(wanted, (m <= row) if source == 0 else (m > row))

            def copy():
                return remote(
                    o2g.at[source], o2w.at[place], o2_ss.at[m, r], o2_rs.at[place], tile, x)

            def own():
                return pltpu.make_async_copy(o2g.at[source], o2w.at[place], o2_rs.at[place])

            if source in go:
                if m in (0, 4):
                    @pl.when(jnp.logical_and(here, c != r))
                    def _():
                        copy().start() if local else copy().wait_send()

                    if local:
                        @pl.when(jnp.logical_and(here, c == r))
                        def _():
                            own().start()
                else:
                    @pl.when(here)
                    def _():
                        copy().start() if local else copy().wait_send()

    for step in range(1, 4):
        other = lax.rem(x + step, 4)
        receive(o2g.at[0, other], og_rs.at[other])
    start(remote(o2g.at[0], o2g.at[1], up_ss, up_rs, t - 8, x), below(8))
    for m in range(4):
        for r in range(2):
            plane_send(m, r, (0,), True)

    def window():
        for m in range(1, 5):
            receive(win.at[2 * m], in_rs.at[2 * m], above(2 * m))

            @pl.when(jnp.logical_or(c == 0, m < 4))
            def _():
                pass_on(m).start()
        for k in range(1, SPAN + 1, 2):
            receive(win.at[k], in_rs.at[k])
        return jnp.concatenate([win[k] for k in range(SPAN + 1)], axis=0)

    def dot(left, right):
        return jnp.dot(left, right, preferred_element_type=F32)

    loads[2].wait()
    wide = window()
    psi = []
    for s in range(2):
        patch = dot(sel[s], wide)
        pr, pi = probe[0].astype(F32), probe[1].astype(F32)
        fr, fi = patch[:, :BLK], patch[:, BLK:]
        psi.append(jnp.concatenate([
            (pr * fr - pi * fi).astype(BF), (pr * fi + pi * fr).astype(BF)], axis=0))
    psi = jnp.concatenate(psi, axis=1)
    for r in range(2):
        for part in range(2):
            at = part * P_SIZE + r * HALF
            half1 = dot(aq[at:at + HALF, :], psi).astype(BF)
            for s in range(2):
                h1[s, part, r * HALF:(r + 1) * HALF, :] = half1[:, s * BLK:(s + 1) * BLK]
        for s in range(2):
            spread(*h1_of(s, r))

    receive(o2g.at[1], up_rs, above(8))
    for m in range(1, 5):
        for r in range(2):
            plane_send(m, r, (1,), True)

    for s in range(2):
        for b, k in enumerate((1, 3, 5, 7, 2, 4, 6, 8, 0)):
            shape = (TH, P_SIZE)
            shifted = lax.broadcasted_iota(jnp.int32, shape, 1) + off_ref[s]
            match = shifted == lax.broadcasted_iota(jnp.int32, shape, 0) + k * TH
            alive = jnp.broadcast_to(cnt_ref[0], shape) > s
            put[b * TH:(b + 1) * TH, s * P_SIZE:(s + 1) * P_SIZE] = jnp.where(
                jnp.logical_and(match, alive), 1.0, 0.0).astype(BF)
    receive(offb.at[d], of_rs)
    shape = (HALF, HALF + TH)
    shifted = lax.broadcasted_iota(jnp.int32, shape, 0).astype(F32) + offb[odd_home][0:1, :HALF + TH]
    match = shifted == lax.broadcasted_iota(jnp.int32, shape, 1).astype(F32)
    psel[...] = jnp.where(match, 1.0, 0.0).astype(BF)
    shape = (HALF + TH, HALF)
    shifted = lax.broadcasted_iota(jnp.int32, shape, 1).astype(F32) + offb[odd_home][0:1, :HALF]
    match = shifted == lax.broadcasted_iota(jnp.int32, shape, 0).astype(F32)
    pput[...] = jnp.where(match, 1.0, 0.0).astype(BF)
    acc[...] = jnp.zeros_like(acc)

    for n in range(4):
        receive(hr.at[n], h1_rs.at[n])
    left = jnp.concatenate([hr[n, part] for part in range(2) for n in range(4)], axis=1)
    for part in range(2):
        for h in range(2):
            at = part * P_SIZE + h * HALF
            ps[part, h] = dot(left, bq[:, at:at + HALF]).astype(BF)
    for k in range(5):
        receive(o2w.at[k], o2_rs.at[k])
    for n in range(4):
        rows = jnp.concatenate([o2w[k, n] for k in range(5)], axis=0)
        o2r[n] = dot(psel[...], rows).astype(BF)

    def second(part, h):
        columns = slice(part * BLK, (part + 1) * BLK)
        return jnp.concatenate([o2r[2 * h, :, columns], o2r[2 * h + 1, :, columns]], axis=1).astype(F32)

    for h in range(2):
        wr, wi = ps[0, h].astype(F32), ps[1, h].astype(F32)
        sr, si = second(0, h), second(1, h)
        ew[:, h * HALF:(h + 1) * HALF] = (wr * sr - wi * si).astype(BF)
        ew[:, P_SIZE + h * HALF:P_SIZE + (h + 1) * HALF] = (wr * si + wi * sr).astype(BF)

    for part in range(2):
        at = pl.multiple_of(part * P_SIZE + d * HALF, HALF)
        gs[part] = dot(ew[...], bf[:, pl.ds(at, HALF)]).astype(BF)
    ex1 = remote(gs, x1.at[c], e1_ss, e1_rs, pair + d, x)
    ex1.start()
    for part in range(2):
        at = pl.multiple_of(part * P_SIZE + c * HALF, HALF)
        x1[c, part] = dot(ew[...], bf[:, pl.ds(at, HALF)]).astype(BF)
    for n in range(4):
        receive(amp.at[n], am_rs.at[n])
    receive(x1.at[d], e1_rs)

    right = jnp.concatenate([x1[r, part] for part in range(2) for r in range(2)], axis=0)
    for r in range(2):
        fr = dot(af[r * HALF:(r + 1) * HALF, :], right)
        fi = dot(af[P_SIZE + r * HALF:P_SIZE + (r + 1) * HALF, :], right)
        measured = jnp.concatenate([amp[2 * r], amp[2 * r + 1]], axis=0).astype(F32)
        keeping = 1.0 - measured / jnp.sqrt(fr * fr + fi * fi + smooth)
        ch[r * HALF:(r + 1) * HALF, :] = (fr * keeping).astype(BF)
        ch[P_SIZE + r * HALF:P_SIZE + (r + 1) * HALF, :] = (fi * keeping).astype(BF)

    for part in range(2):
        at = pl.multiple_of(part * P_SIZE + d * HALF, HALF)
        ks[part] = dot(bf[pl.ds(at, HALF), :], ch[...]).astype(BF)
    ex2 = remote(ks, y.at[c], e2_ss, e2_rs, pair + d, x)
    ex2.start()
    for part in range(2):
        at = pl.multiple_of(part * P_SIZE + c * HALF, HALF)
        y[c, part] = dot(bf[pl.ds(at, HALF), :], ch[...]).astype(BF)
    receive(y.at[d], e2_rs)

    left = jnp.concatenate([y[h, part] for part in range(2) for h in range(2)], axis=1)
    for h in range(2):
        er = dot(left, af[:, h * HALF:(h + 1) * HALF])
        ei = dot(left, af[:, P_SIZE + h * HALF:P_SIZE + (h + 1) * HALF])
        wr, wi = ps[0, h].astype(F32), ps[1, h].astype(F32)
        sr, si = second(0, h), second(1, h)
        tr, ti = (wr * er + wi * ei).astype(BF), (wr * ei - wi * er).astype(BF)
        for n in range(2):
            t2s[2 * h + n, :, :BLK] = tr[:, n * BLK:(n + 1) * BLK]
            t2s[2 * h + n, :, BLK:] = ti[:, n * BLK:(n + 1) * BLK]
        gw[:, h * HALF:(h + 1) * HALF] = (sr * er + si * ei).astype(BF)
        gw[:, P_SIZE + h * HALF:P_SIZE + (h + 1) * HALF] = (sr * ei - si * er).astype(BF)

    for n in range(4):
        moved = dot(pput[...], t2s[n]).astype(BF)
        for k in range(5):
            t2o[k, n] = moved[k * TH:(k + 1) * TH]

    def term_send(k, kind, begin):
        place = k + odd_home + 4 * c
        m = place // 2
        core = lax.rem(place, 2)
        tile = plane + 2 * lax.rem(row + m, 4) + core
        copy = remote(t2o.at[k], rin.at[m, c], rt_ss.at[k], rt_rs.at[m, c], tile, x)
        here = (row + m > 3) if kind else (row + m <= 3)

        @pl.when(jnp.logical_and(here, tile != t))
        def _():
            copy.start() if begin else copy.wait_send()

        if begin:
            @pl.when(jnp.logical_and(here, tile == t))
            def _():
                pltpu.make_async_copy(t2o.at[k], rin.at[m, c], rt_rs.at[m, c]).start()

    def term_take(m, r, kind):
        place = 2 * m + c - odd_home - 4 * r
        here = (m > row) if kind else (m <= row)

        @pl.when(jnp.logical_and(here, jnp.logical_and(place >= 0, place <= 4)))
        def _():
            receive(rin.at[m, r], rt_rs.at[m, r])
            acc[kind] += rin[m, r].astype(F32)

    for k in reversed(range(5)):
        term_send(k, 1, True)
    for k in reversed(range(5)):
        term_send(k, 0, True)

    def is_home(n):
        return jnp.logical_and(home == t, x == n)

    def give(src, dst, ss, rs, n):
        where = dst.at[slot, :, pl.ds(pl.multiple_of(c * HALF, HALF), HALF), :]

        @pl.when(is_home(n))
        def _():
            pltpu.make_async_copy(src.at[n], where, rs.at[slot, c]).start()

        @pl.when(jnp.logical_not(is_home(n)))
        def _():
            remote(src.at[n], where, ss.at[n], rs.at[slot, c], home, n).start()

    def give_wait(src, dst, ss, rs, n):
        where = dst.at[slot, :, pl.ds(pl.multiple_of(c * HALF, HALF), HALF), :]

        @pl.when(jnp.logical_not(is_home(n)))
        def _():
            remote(src.at[n], where, ss.at[n], rs.at[slot, c], home, n).wait_send()

    for h in range(2):
        for part in range(2):
            at = part * P_SIZE + h * HALF
            back2 = dot(gw[...], aq[:, at:at + HALF]).astype(BF)
            for n in range(2):
                b2s[2 * h + n, part] = back2[:, n * BLK:(n + 1) * BLK]
        for n in range(2):
            give(b2s, b2r, b2_ss, b2_rs, 2 * h + n)

    for m in reversed(range(1, 5)):
        for r in range(2):
            term_take(m, r, 1)
    uo[...] = acc[1].astype(BF)
    start(remote(uo, ui, uu_ss, uu_rs, t + 8, x), above(8))

    for s in range(2):
        for r in range(2):
            receive(b2r.at[s, :, pl.ds(r * HALF, HALF), :], b2_rs.at[s, r])
    right = jnp.concatenate([
        jnp.concatenate([b2r[0, part], b2r[1, part]], axis=1) for part in range(2)], axis=0)
    for r in range(2):
        nr = dot(bq[r * HALF:(r + 1) * HALF, :], right)
        ni = dot(bq[P_SIZE + r * HALF:P_SIZE + (r + 1) * HALF, :], right)
        pr = probe[0, r * HALF:(r + 1) * HALF, :].astype(F32)
        pi = probe[1, r * HALF:(r + 1) * HALF, :].astype(F32)
        for s in range(2):
            sr, si = nr[:, s * BLK:(s + 1) * BLK], ni[:, s * BLK:(s + 1) * BLK]
            rows = slice(s * P_SIZE + r * HALF, s * P_SIZE + (r + 1) * HALF)
            tp[rows, :BLK] = (pr * sr + pi * si).astype(BF)
            tp[rows, BLK:] = (pr * si - pi * sr).astype(BF)

    def collect(which, terms):
        total = dot(put[:HALF, :], terms)
        for m in range(4):
            odd[which, m] = total[m * TH:(m + 1) * TH].astype(BF)
            start(remote(
                odd.at[which, m], got.at[which, m], od_ss.at[which, m], od_rs.at[which, m],
                pair + d, x))
        total = dot(put[HALF:, :], terms)
        for m in range(1, 5):
            even[which, m] = total[(m - 1) * TH:m * TH]
        even[which, 0] = total[HALF:]

    def hand_on(which):
        for m in range(4):
            receive(got.at[which, m], od_rs.at[which, m])
            even[which, m + d] += got[which, m].astype(F32)
        for m in range(1, 5):
            outs[which, m] = even[which, m].astype(BF)
            start(remote(
                outs.at[which, m], oin.at[which, m], out_ss.at[which, m],
                out_rs.at[which, m], t + 2 * m, x), above(2 * m))

    collect(0, tp[...])
    hand_on(0)
    for m in range(4):
        for r in range(2):
            term_take(m, r, 0)
    receive(ui, uu_rs, below(8))
    acc[0] += ui[...].astype(F32)
    xo[...] = acc[0].astype(BF)
    for step in range(1, 4):
        other = lax.rem(x + step, 4)
        start(remote(xo.at[other], xi.at[x], xs_ss.at[step - 1], xs_rs.at[x], t, other))

    total = even[0, 0]
    for m in range(1, 5):
        receive(oin.at[0, m], out_rs.at[0, m], below(2 * m))
        total = total + oin[0, m].astype(F32)
    for part in range(2):
        out_ref[0, part] = total[:, part * BLK:(part + 1) * BLK]

    total = acc[0, x]
    for step in range(1, 4):
        other = lax.rem(x + step, 4)
        receive(xi.at[other], xs_rs.at[other])
        total = total + xi[other].astype(F32)
    for part in range(2):
        out_ref[1, part] = total[:, part * BLK:(part + 1) * BLK]

    for copy, here in sends:
        if here is None:
            copy.wait_send()
        else:
            pl.when(here)(copy.wait_send)
    for m in range(5):
        @pl.when((c == 1) if m == 0 else jnp.logical_or(c == 0, m < 4))
        def _():
            pass_on(m).wait_send()
        for r in range(2):
            plane_send(m, r, (0, 1), False)
    for k in range(5):
        term_send(k, 0, False)
        term_send(k, 1, False)
    ex1.wait_send()
    ex2.wait_send()
    for s in range(2):
        for r in range(2):
            spread_wait(*amp_of(s, r))
            spread_wait(*h1_of(s, r))
    for n in range(4):
        give_wait(b2s, b2r, b2_ss, b2_rs, n)


def shards(tiles, far, near, object_slab, probe_wave, amplitudes, row_offsets, position_counts):
    dma = pltpu.SemaphoreType.DMA
    vmem = pltpu.VMEM
    n2 = 2 * P_SIZE
    scratch = [
        pltpu.SMEM((2,), jnp.int32), pltpu.SMEM((1,), jnp.int32),
        vmem((2, 2, TH, BLK), F32),
        vmem((2, P_SIZE, BLK), BF),
        vmem((2, BLK, P_SIZE), F32),
        vmem((n2, n2), BF), vmem((n2, n2), BF), vmem((n2, n2), BF), vmem((n2, n2), BF),
        vmem((SPAN + 1, TH, HALF), BF),
        vmem((2, 4, TH, HALF), BF),
        vmem((5, 4, TH, HALF), BF),
        vmem((2, 8, 3 * BLK), F32),
        vmem((2, P_SIZE, P_SIZE + TH), BF),
        vmem((HALF, HALF + TH), BF),
        vmem((P_SIZE + TH, n2), BF),
        vmem((2, 2, P_SIZE, BLK), BF),
        vmem((2, 2, BLK, HALF), BF),
        vmem((4, 2, HALF, BLK), BF),
        vmem((4, HALF, HALF), BF),
        vmem((4, BLK, HALF), BF),
        vmem((2, 2, HALF, HALF), BF),
        vmem((HALF, n2), BF),
        vmem((2, HALF, HALF), BF),
        vmem((2, 2, HALF, HALF), BF),
        vmem((n2, HALF), BF),
        vmem((2, HALF, HALF), BF),
        vmem((2, 2, HALF, HALF), BF),
        vmem((4, HALF, HALF), BF),
        vmem((HALF, n2), BF),
        vmem((4, 2, HALF, BLK), BF),
        vmem((2, 2, P_SIZE, BLK), BF),
        vmem((n2, HALF), BF),
        vmem((2, 4, TH, HALF), BF),
        vmem((2, 4, TH, HALF), BF),
        vmem((2, 5, TH, HALF), F32),
        vmem((2, 5, TH, HALF), BF),
        vmem((2, 5, TH, HALF), BF),
        vmem((HALF + TH, HALF), BF),
        vmem((5, 4, TH, HALF), BF),
        vmem((5, 2, 4, TH, HALF), BF),
        vmem((2, 4, TH, HALF), F32),
        vmem((4, TH, HALF), BF), vmem((4, TH, HALF), BF),
        vmem((4, TH, HALF), BF), vmem((4, TH, HALF), BF),
        dma((5,)), dma((4, 3)),
        dma((5,)), dma((SPAN + 1,)), dma((5,)), dma((3,)), dma((4,)), dma, dma, dma, dma,
        dma((2, 2)), dma((4,)), dma((5, 2)), dma((5,)), dma((2, 2)), dma((4,)),
        dma, dma, dma, dma,
        dma((4,)), dma((2, 2)), dma((5,)), dma((5, 2)), dma, dma, dma((3,)), dma((4,)),
        dma((2, 4)), dma((2, 4)), dma((2, 5)), dma((2, 5)),
    ]
    any_spec = pl.BlockSpec(memory_space=pl.ANY)
    return pl.pallas_call(
        functools.partial(body, tiles),
        out_shape=jax.ShapeDtypeStruct(object_slab.shape, F32),
        in_specs=[any_spec] * 7,
        out_specs=pl.BlockSpec(memory_space=pltpu.VMEM),
        scratch_shapes=scratch,
        compiler_params=pltpu.CompilerParams(
            collective_id=0, has_side_effects=True, vmem_limit_bytes=56_300_000
        ),
        name="object_gradient",
    )(row_offsets, position_counts, object_slab, probe_wave, amplitudes, near, far)


def solution(mesh):
    in_specs = (
        P(None, None, "tile", "scan"),
        P(None, None, "scan"),
        P("tile", "scan", None),
        P("tile"),
        P("tile"),
    )
    out_specs = P(None, None, "tile", "scan")
    far, near = tables()
    run = functools.partial(shards, mesh.shape["tile"], far, near)
    return jax.shard_map(run, mesh=mesh, in_specs=in_specs, out_specs=out_specs, check_vma=False)
```

```python
import functools
import math

import jax
import jax.numpy as jnp
import numpy as np
from jax import lax
from jax.experimental import pallas as pl
from jax.experimental.pallas import tpu as pltpu
from jax.sharding import PartitionSpec as P

P_SIZE = 512
HALF = 256
BLK = 128
TH = 64
SPAN = P_SIZE // TH

fresnel = 0.5
smooth = 1.0
MESH = pl.DeviceIdType.MESH
BF = jnp.bfloat16
F32 = jnp.float32


def tables():
    index = np.arange(P_SIZE)
    angles = 2.0 * np.pi / P_SIZE * (index[:, None] * index[None, :] % P_SIZE)
    wave = np.exp(1j * angles)
    far = np.conj(wave) / math.sqrt(P_SIZE)
    centred = np.where(index < P_SIZE // 2, index, index - P_SIZE).astype(np.float64)
    kernel = np.exp(-1j * np.pi * fresnel / P_SIZE * centred * centred)
    near = (wave * kernel[None, :]) @ np.conj(wave).T / P_SIZE

    def planes(table):
        both = np.stack([table.real, table.imag])
        return both.astype(np.float32).astype(BF)

    return planes(far), planes(near)


def body(
    tiles,
    off_hbm, cnt_hbm, slab_hbm, probe_hbm, amp_hbm, tq_hbm, tf_hbm,
    out_ref,
    off_ref, cnt_ref, slab, probe, ampf, aq, bq, af, bf,
    win, o2g, o2w, offb, sel, psel, put, h1, ampb, hr, o2r, amp,
    ps, ew, gs, x1, ch, ks, y, t2s, gw, b2s, b2r, tp, odd, got, even, outs, oin,
    pput, t2o, rin, acc, uo, ux, us, ui, xo, xi, mine,
    loc_sem, tab_sem,
    in_ss, in_rs, fw_ss, og_ss, og_rs, up_ss, up_rs, of_ss, of_rs,
    h1_ss, h1_rs, o2_ss, o2_rs, am_ss, am_rs,
    e1_ss, e1_rs, e2_ss, e2_rs, b2_ss, b2_rs, rt_ss, rt_rs, uu_ss, uu_rs, xs_ss, xs_rs, od_ss, od_rs, out_ss, out_rs,
):
    t = lax.axis_index("tile")
    x = lax.axis_index("scan")
    c = lax.rem(t, 2)
    d = 1 - c
    pair = t - c
    home = pair + lax.rem(x, 2)
    slot = x // 2
    odd_home = lax.rem(x, 2)
    row = lax.rem(t // 2, 4)
    plane = t - lax.rem(t, 8)

    def remote(src, dst, ss, rs, tile, scan):
        return pltpu.make_async_remote_copy(
            src_ref=src, dst_ref=dst, send_sem=ss, recv_sem=rs,
            device_id={"tile": tile, "scan": scan}, device_id_type=MESH,
        )

    loads = [
        pltpu.make_async_copy(slab_hbm, slab, loc_sem.at[0]),
        pltpu.make_async_copy(amp_hbm, ampf, loc_sem.at[1]),
        pltpu.make_async_copy(probe_hbm, probe, loc_sem.at[2]),
        pltpu.make_async_copy(off_hbm, off_ref, loc_sem.at[3]),
        pltpu.make_async_copy(cnt_hbm, cnt_ref, loc_sem.at[4]),
    ]
    for load in loads:
        load.start()

    barrier = pltpu.get_barrier_semaphore()

    def greet(tile, scan):
        pl.semaphore_signal(
            barrier, inc=1, device_id={"tile": tile, "scan": scan}, device_id_type=MESH
        )

    for n in range(1, 8):
        greet(plane + lax.rem(t + n, 8), x)
    def below(k):
        return t - k >= 0

    def above(k):
        return t + k < tiles

    for k in range(2, SPAN + 1, 2):
        @pl.when(above(k))
        def _():
            greet(t + k, x)

        @pl.when(below(k))
        def _():
            greet(t - k, x)
    for step in range(1, 4):
        for core in range(2):
            greet(pair + core, lax.rem(x + step, 4))

    def table_loads(src, dst, which, column):
        copies = []
        for n, (up, left, plane) in enumerate([(0, 0, 0), (1 - column, column, 1), (1, 1, 0)]):
            where = dst.at[pl.ds(up * P_SIZE, P_SIZE), pl.ds(left * P_SIZE, P_SIZE)]
            copies.append(pltpu.make_async_copy(src.at[plane], where, tab_sem.at[which, n]))
        for copy in copies:
            copy.start()
        return copies

    def table_ready(dst, copies, column):
        for copy in copies:
            copy.wait()
        imag = dst[(1 - column) * P_SIZE:(2 - column) * P_SIZE, column * P_SIZE:(column + 1) * P_SIZE]
        dst[column * P_SIZE:(column + 1) * P_SIZE, (1 - column) * P_SIZE:(2 - column) * P_SIZE] = -imag

    aq_loads = table_loads(tq_hbm, aq, 0, 0)
    bq_loads = table_loads(tq_hbm, bq, 1, 1)
    bf_loads = table_loads(tf_hbm, bf, 2, 1)
    af_loads = table_loads(tf_hbm, af, 3, 0)

    loads[0].wait()
    for part in range(2):
        win[0, :, part * BLK:(part + 1) * BLK] = slab[0, part].astype(BF)
        o2g[0, x, :, part * BLK:(part + 1) * BLK] = slab[1, part].astype(BF)
    loads[3].wait()
    loads[4].wait()
    shape = (8, 3 * BLK)
    offset = jnp.broadcast_to(off_ref[slot], shape)
    alive = jnp.broadcast_to(cnt_ref[0], shape) > jnp.broadcast_to(slot, shape)
    offb[c] = jnp.where(alive, offset, -2 * P_SIZE).astype(F32)

    for m in range(1, 5):
        @pl.when(jnp.logical_not(above(2 * m)))
        def _():
            win[2 * m] = jnp.zeros((TH, HALF), BF)

        @pl.when(jnp.logical_not(below(2 * m)))
        def _():
            oin[0, m] = jnp.zeros((TH, HALF), BF)

    @pl.when(jnp.logical_not(above(8)))
    def _():
        o2g[1, x] = jnp.zeros((TH, HALF), BF)

    @pl.when(jnp.logical_not(below(8)))
    def _():
        ui[...] = jnp.zeros((TH, HALF), BF)

    pl.semaphore_wait(
        barrier, 13 + jnp.minimum(4, (tiles - 1 - t) // 2) + jnp.minimum(4, t // 2))

    sends = []

    def start(copy, here=None):
        sends.append((copy, here))
        if here is None:
            copy.start()
        else:
            pl.when(here)(copy.start)

    def receive(dst, rs, here=None):
        copy = pltpu.make_async_copy(dst, dst, rs)
        if here is None:
            copy.wait()
        else:
            pl.when(here)(copy.wait)

    for k in range(2, SPAN + 1, 2):
        start(remote(
            win.at[0], win.at[k], in_ss.at[k // 2], in_rs.at[k], t - k, x), below(k))

    start(remote(o2g.at[0, x], o2g.at[1, x], up_ss, up_rs, t - 8, x), below(8))

    def pass_on(m):
        k = 2 * m - 1 + 2 * c
        return remote(win.at[2 * m], win.at[k], fw_ss.at[m], in_rs.at[k], pair + d, x)

    @pl.when(c == 1)
    def _():
        pass_on(0).start()

    def gather(source):
        for step in range(1, 4):
            start(remote(
                o2g.at[source, x], o2g.at[source, x], og_ss.at[source, step - 1],
                og_rs.at[source, x], t, lax.rem(x + step, 4)))

    def gathered(source):
        for step in range(1, 4):
            other = lax.rem(x + step, 4)
            receive(o2g.at[source, other], og_rs.at[source, other])

    gather(0)
    start(remote(offb.at[c], offb.at[c], of_ss, of_rs, pair + d, x))

    for s in range(2):
        shape = (P_SIZE, P_SIZE + TH)
        shifted = lax.broadcasted_iota(jnp.int32, shape, 0) + off_ref[s]
        match = shifted == lax.broadcasted_iota(jnp.int32, shape, 1)
        sel[s] = jnp.where(match, 1.0, 0.0).astype(BF)
    loads[1].wait()
    for s in range(2):
        for r in range(2):
            ampb[s, r] = ampf[s, :, r * HALF:(r + 1) * HALF].astype(BF)

    def is_self(s, r):
        return jnp.logical_and(2 * s + c == x, c == r)

    def spread(src, dst, ss, rs, s, r):
        mine = is_self(s, r)

        @pl.when(mine)
        def _():
            pltpu.make_async_copy(src, dst.at[x], rs.at[x]).start()

        @pl.when(jnp.logical_not(mine))
        def _():
            remote(src, dst.at[x], ss.at[s, r], rs.at[x], pair + r, 2 * s + c).start()

    def spread_wait(src, dst, ss, rs, s, r):
        @pl.when(jnp.logical_not(is_self(s, r)))
        def _():
            remote(src, dst.at[x], ss.at[s, r], rs.at[x], pair + r, 2 * s + c).wait_send()

    def amp_of(s, r):
        return ampb.at[s, r], amp, am_ss, am_rs, s, r

    def h1_of(s, r):
        return h1.at[s, :, pl.ds(r * HALF, HALF), :], hr, h1_ss, h1_rs, s, r

    for s in range(2):
        for r in range(2):
            spread(*amp_of(s, r))

    table_ready(aq, aq_loads, 0)
    table_ready(bq, bq_loads, 1)
    table_ready(bf, bf_loads, 1)
    table_ready(af, af_loads, 0)

    def plane_send(m, r, go, local):
        place = 2 * m + c - odd_home - 4 * r
        wanted = jnp.logical_and(place >= 0, place <= 4)
        for source in range(2):
            if m in (0, 4):
                if source != m // 4:
                    continue
                tile, here = pair + r, wanted
            else:
                tile = plane + 2 * lax.rem(row - m + 4, 4) + r
                here = jnp.logical_and(wanted, (m <= row) if source == 0 else (m > row))

            def copy():
                return remote(
                    o2g.at[source], o2w.at[place], o2_ss.at[m, r], o2_rs.at[place], tile, x)

            def own():
                return pltpu.make_async_copy(o2g.at[source], o2w.at[place], o2_rs.at[place])

            if source in go:
                if m in (0, 4):
                    @pl.when(jnp.logical_and(here, c != r))
                    def _():
                        copy().start() if local else copy().wait_send()

                    if local:
                        @pl.when(jnp.logical_and(here, c == r))
                        def _():
                            own().start()
                else:
                    @pl.when(here)
                    def _():
                        copy().start() if local else copy().wait_send()

    def take_tile(m, here, exists=None):
        receive(win.at[2 * m], in_rs.at[2 * m], here if exists is None else jnp.logical_and(here, exists))

        @pl.when(jnp.logical_and(here, jnp.logical_or(c == 0, m < 4)))
        def _():
            pass_on(m).start()

    for m in range(1, 4):
        take_tile(m, row + m <= 3)
    for m in range(1, 5):
        take_tile(m, row + m > 3, above(2 * m))
    receive(o2g.at[1, x], up_rs, above(8))
    gather(1)
    gathered(0)
    for m in range(4):
        for r in range(2):
            plane_send(m, r, (0,), True)

    def dot(left, right):
        return jnp.dot(left, right, preferred_element_type=F32)

    loads[2].wait()
    for k in range(1, SPAN + 1, 2):
        receive(win.at[k], in_rs.at[k])
    wide = jnp.concatenate([win[k] for k in range(SPAN + 1)], axis=0)
    psi = []
    for s in range(2):
        patch = dot(sel[s], wide)
        pr, pi = probe[0].astype(F32), probe[1].astype(F32)
        fr, fi = patch[:, :BLK], patch[:, BLK:]
        psi.append(jnp.concatenate([
            (pr * fr - pi * fi).astype(BF), (pr * fi + pi * fr).astype(BF)], axis=0))
    psi = jnp.concatenate(psi, axis=1)
    for r in range(2):
        for part in range(2):
            at = part * P_SIZE + r * HALF
            half1 = dot(aq[at:at + HALF, :], psi).astype(BF)
            for s in range(2):
                h1[s, part, r * HALF:(r + 1) * HALF, :] = half1[:, s * BLK:(s + 1) * BLK]
        for s in range(2):
            spread(*h1_of(s, r))

    gathered(1)
    for m in range(1, 5):
        for r in range(2):
            plane_send(m, r, (1,), True)

    for s in range(2):
        for b, k in enumerate((1, 3, 5, 7, 2, 4, 6, 8, 0)):
            shape = (TH, P_SIZE)
            shifted = lax.broadcasted_iota(jnp.int32, shape, 1) + off_ref[s]
            match = shifted == lax.broadcasted_iota(jnp.int32, shape, 0) + k * TH
            alive = jnp.broadcast_to(cnt_ref[0], shape) > s
            put[b * TH:(b + 1) * TH, s * P_SIZE:(s + 1) * P_SIZE] = jnp.where(
                jnp.logical_and(match, alive), 1.0, 0.0).astype(BF)
    receive(offb.at[d], of_rs)
    shape = (HALF, HALF + TH)
    shifted = lax.broadcasted_iota(jnp.int32, shape, 0).astype(F32) + offb[odd_home][0:1, :HALF + TH]
    match = shifted == lax.broadcasted_iota(jnp.int32, shape, 1).astype(F32)
    psel[...] = jnp.where(match, 1.0, 0.0).astype(BF)
    shape = (HALF + TH, HALF)
    shifted = lax.broadcasted_iota(jnp.int32, shape, 1).astype(F32) + offb[odd_home][0:1, :HALF]
    match = shifted == lax.broadcasted_iota(jnp.int32, shape, 0).astype(F32)
    pput[...] = jnp.where(match, 1.0, 0.0).astype(BF)
    acc[...] = jnp.zeros_like(acc)

    for n in range(4):
        receive(hr.at[n], h1_rs.at[n])
    left = jnp.concatenate([hr[n, part] for part in range(2) for n in range(4)], axis=1)
    for part in range(2):
        for h in range(2):
            at = part * P_SIZE + h * HALF
            ps[part, h] = dot(left, bq[:, at:at + HALF]).astype(BF)
    for k in range(5):
        receive(o2w.at[k], o2_rs.at[k])
    for n in range(4):
        rows = jnp.concatenate([o2w[k, n] for k in range(5)], axis=0)
        o2r[n] = dot(psel[...], rows).astype(BF)

    def second(part, h):
        columns = slice(part * BLK, (part + 1) * BLK)
        return jnp.concatenate([o2r[2 * h, :, columns], o2r[2 * h + 1, :, columns]], axis=1).astype(F32)

    for h in range(2):
        wr, wi = ps[0, h].astype(F32), ps[1, h].astype(F32)
        sr, si = second(0, h), second(1, h)
        ew[:, h * HALF:(h + 1) * HALF] = (wr * sr - wi * si).astype(BF)
        ew[:, P_SIZE + h * HALF:P_SIZE + (h + 1) * HALF] = (wr * si + wi * sr).astype(BF)

    for part in range(2):
        at = pl.multiple_of(part * P_SIZE + d * HALF, HALF)
        gs[part] = dot(ew[...], bf[:, pl.ds(at, HALF)]).astype(BF)
    ex1 = remote(gs, x1.at[c], e1_ss, e1_rs, pair + d, x)
    ex1.start()
    for part in range(2):
        at = pl.multiple_of(part * P_SIZE + c * HALF, HALF)
        x1[c, part] = dot(ew[...], bf[:, pl.ds(at, HALF)]).astype(BF)
    def near_rows(which, at):
        left = jnp.concatenate([
            af[at:at + HALF, pl.ds(pl.multiple_of(part * P_SIZE + which * HALF, HALF), HALF)]
            for part in range(2)], axis=1)
        return dot(left, jnp.concatenate([x1[which, part] for part in range(2)], axis=0))

    for n in range(4):
        mine[n] = near_rows(c, n * HALF)
    for n in range(4):
        receive(amp.at[n], am_rs.at[n])
    receive(x1.at[d], e1_rs)
    for r in range(2):
        fr = mine[r] + near_rows(d, r * HALF)
        fi = mine[2 + r] + near_rows(d, P_SIZE + r * HALF)
        measured = jnp.concatenate([amp[2 * r], amp[2 * r + 1]], axis=0).astype(F32)
        keeping = 1.0 - measured / jnp.sqrt(fr * fr + fi * fi + smooth)
        ch[r * HALF:(r + 1) * HALF, :] = (fr * keeping).astype(BF)
        ch[P_SIZE + r * HALF:P_SIZE + (r + 1) * HALF, :] = (fi * keeping).astype(BF)

    for part in range(2):
        at = pl.multiple_of(part * P_SIZE + d * HALF, HALF)
        ks[part] = dot(bf[pl.ds(at, HALF), :], ch[...]).astype(BF)
    ex2 = remote(ks, y.at[c], e2_ss, e2_rs, pair + d, x)
    ex2.start()
    for part in range(2):
        at = pl.multiple_of(part * P_SIZE + c * HALF, HALF)
        y[c, part] = dot(bf[pl.ds(at, HALF), :], ch[...]).astype(BF)
    def near_columns(which, at):
        right = jnp.concatenate([
            af[pl.ds(pl.multiple_of(part * P_SIZE + which * HALF, HALF), HALF), at:at + HALF]
            for part in range(2)], axis=0)
        return dot(jnp.concatenate([y[which, part] for part in range(2)], axis=1), right)

    for n in range(4):
        mine[n] = near_columns(c, n * HALF)
    receive(y.at[d], e2_rs)
    for h in range(2):
        er = mine[h] + near_columns(d, h * HALF)
        ei = mine[2 + h] + near_columns(d, P_SIZE + h * HALF)
        wr, wi = ps[0, h].astype(F32), ps[1, h].astype(F32)
        sr, si = second(0, h), second(1, h)
        tr, ti = (wr * er + wi * ei).astype(BF), (wr * ei - wi * er).astype(BF)
        for n in range(2):
            t2s[2 * h + n, :, :BLK] = tr[:, n * BLK:(n + 1) * BLK]
            t2s[2 * h + n, :, BLK:] = ti[:, n * BLK:(n + 1) * BLK]
        gw[:, h * HALF:(h + 1) * HALF] = (sr * er + si * ei).astype(BF)
        gw[:, P_SIZE + h * HALF:P_SIZE + (h + 1) * HALF] = (sr * ei - si * er).astype(BF)

    for n in range(4):
        moved = dot(pput[...], t2s[n]).astype(BF)
        for k in range(5):
            t2o[k, n] = moved[k * TH:(k + 1) * TH]

    def term_send(k, kind, begin):
        place = k + odd_home + 4 * c
        m = place // 2
        core = lax.rem(place, 2)
        tile = plane + 2 * lax.rem(row + m, 4) + core
        copy = remote(t2o.at[k], rin.at[m, c], rt_ss.at[k], rt_rs.at[m, c], tile, x)
        here = (row + m > 3) if kind else (row + m <= 3)

        @pl.when(jnp.logical_and(here, tile != t))
        def _():
            copy.start() if begin else copy.wait_send()

        if begin:
            @pl.when(jnp.logical_and(here, tile == t))
            def _():
                pltpu.make_async_copy(t2o.at[k], rin.at[m, c], rt_rs.at[m, c]).start()

    def term_take(m, r, kind):
        place = 2 * m + c - odd_home - 4 * r
        here = (m > row) if kind else (m <= row)

        @pl.when(jnp.logical_and(here, jnp.logical_and(place >= 0, place <= 4)))
        def _():
            receive(rin.at[m, r], rt_rs.at[m, r])
            acc[kind] += rin[m, r].astype(F32)

    for k in reversed(range(5)):
        term_send(k, 1, True)
    for k in reversed(range(5)):
        term_send(k, 0, True)

    def is_home(n):
        return jnp.logical_and(home == t, x == n)

    def give(src, dst, ss, rs, n):
        where = dst.at[slot, :, pl.ds(pl.multiple_of(c * HALF, HALF), HALF), :]

        @pl.when(is_home(n))
        def _():
            pltpu.make_async_copy(src.at[n], where, rs.at[slot, c]).start()

        @pl.when(jnp.logical_not(is_home(n)))
        def _():
            remote(src.at[n], where, ss.at[n], rs.at[slot, c], home, n).start()

    def give_wait(src, dst, ss, rs, n):
        where = dst.at[slot, :, pl.ds(pl.multiple_of(c * HALF, HALF), HALF), :]

        @pl.when(jnp.logical_not(is_home(n)))
        def _():
            remote(src.at[n], where, ss.at[n], rs.at[slot, c], home, n).wait_send()

    for h in range(2):
        for part in range(2):
            at = part * P_SIZE + h * HALF
            back2 = dot(gw[...], aq[:, at:at + HALF]).astype(BF)
            for n in range(2):
                b2s[2 * h + n, part] = back2[:, n * BLK:(n + 1) * BLK]
        for n in range(2):
            give(b2s, b2r, b2_ss, b2_rs, 2 * h + n)

    for s in range(2):
        for r in range(2):
            receive(b2r.at[s, :, pl.ds(r * HALF, HALF), :], b2_rs.at[s, r])
    right = jnp.concatenate([
        jnp.concatenate([b2r[0, part], b2r[1, part]], axis=1) for part in range(2)], axis=0)
    for r in range(2):
        nr = dot(bq[r * HALF:(r + 1) * HALF, :], right)
        ni = dot(bq[P_SIZE + r * HALF:P_SIZE + (r + 1) * HALF, :], right)
        pr = probe[0, r * HALF:(r + 1) * HALF, :].astype(F32)
        pi = probe[1, r * HALF:(r + 1) * HALF, :].astype(F32)
        for s in range(2):
            sr, si = nr[:, s * BLK:(s + 1) * BLK], ni[:, s * BLK:(s + 1) * BLK]
            rows = slice(s * P_SIZE + r * HALF, s * P_SIZE + (r + 1) * HALF)
            tp[rows, :BLK] = (pr * sr + pi * si).astype(BF)
            tp[rows, BLK:] = (pr * si - pi * sr).astype(BF)

    def collect(which, terms):
        total = dot(put[:HALF, :], terms)
        for m in range(4):
            odd[which, m] = total[m * TH:(m + 1) * TH].astype(BF)
            start(remote(
                odd.at[which, m], got.at[which, m], od_ss.at[which, m], od_rs.at[which, m],
                pair + d, x))
        total = dot(put[HALF:, :], terms)
        for m in range(1, 5):
            even[which, m] = total[(m - 1) * TH:m * TH]
        even[which, 0] = total[HALF:]

    def hand_on(which):
        for m in range(4):
            receive(got.at[which, m], od_rs.at[which, m])
            even[which, m + d] += got[which, m].astype(F32)
        for m in range(1, 5):
            outs[which, m] = even[which, m].astype(BF)
            start(remote(
                outs.at[which, m], oin.at[which, m], out_ss.at[which, m],
                out_rs.at[which, m], t + 2 * m, x), above(2 * m))

    collect(0, tp[...])
    for m in reversed(range(1, 5)):
        for r in range(2):
            term_take(m, r, 1)
    uo[...] = acc[1].astype(BF)
    for step in range(1, 4):
        other = lax.rem(x + step, 4)
        start(remote(uo.at[other], ux.at[x], xs_ss.at[1, step - 1], xs_rs.at[1, x], t, other))
    hand_on(0)
    for m in range(4):
        for r in range(2):
            term_take(m, r, 0)
    xo[...] = acc[0].astype(BF)
    for step in range(1, 4):
        other = lax.rem(x + step, 4)
        start(remote(xo.at[other], xi.at[x], xs_ss.at[0, step - 1], xs_rs.at[0, x], t, other))

    total = acc[1, x]
    for step in range(1, 4):
        other = lax.rem(x + step, 4)
        receive(ux.at[other], xs_rs.at[1, other])
        total = total + ux[other].astype(F32)
    us[...] = total.astype(BF)
    start(remote(us, ui, uu_ss, uu_rs, t + 8, x), above(8))

    total = even[0, 0]
    for m in range(1, 5):
        receive(oin.at[0, m], out_rs.at[0, m], below(2 * m))
        total = total + oin[0, m].astype(F32)
    for part in range(2):
        out_ref[0, part] = total[:, part * BLK:(part + 1) * BLK]

    total = acc[0, x]
    for step in range(1, 4):
        other = lax.rem(x + step, 4)
        receive(xi.at[other], xs_rs.at[0, other])
        total = total + xi[other].astype(F32)
    receive(ui, uu_rs, below(8))
    total = total + ui[...].astype(F32)
    for part in range(2):
        out_ref[1, part] = total[:, part * BLK:(part + 1) * BLK]

    for copy, here in sends:
        if here is None:
            copy.wait_send()
        else:
            pl.when(here)(copy.wait_send)
    for m in range(5):
        @pl.when((c == 1) if m == 0 else jnp.logical_or(c == 0, m < 4))
        def _():
            pass_on(m).wait_send()
        for r in range(2):
            plane_send(m, r, (0, 1), False)
    for k in range(5):
        term_send(k, 0, False)
        term_send(k, 1, False)
    ex1.wait_send()
    ex2.wait_send()
    for s in range(2):
        for r in range(2):
            spread_wait(*amp_of(s, r))
            spread_wait(*h1_of(s, r))
    for n in range(4):
        give_wait(b2s, b2r, b2_ss, b2_rs, n)


def shards(tiles, far, near, object_slab, probe_wave, amplitudes, row_offsets, position_counts):
    dma = pltpu.SemaphoreType.DMA
    vmem = pltpu.VMEM
    n2 = 2 * P_SIZE
    scratch = [
        pltpu.SMEM((2,), jnp.int32), pltpu.SMEM((1,), jnp.int32),
        vmem((2, 2, TH, BLK), F32),
        vmem((2, P_SIZE, BLK), BF),
        vmem((2, BLK, P_SIZE), F32),
        vmem((n2, n2), BF), vmem((n2, n2), BF), vmem((n2, n2), BF), vmem((n2, n2), BF),
        vmem((SPAN + 1, TH, HALF), BF),
        vmem((2, 4, TH, HALF), BF),
        vmem((5, 4, TH, HALF), BF),
        vmem((2, 8, 3 * BLK), F32),
        vmem((2, P_SIZE, P_SIZE + TH), BF),
        vmem((HALF, HALF + TH), BF),
        vmem((P_SIZE + TH, n2), BF),
        vmem((2, 2, P_SIZE, BLK), BF),
        vmem((2, 2, BLK, HALF), BF),
        vmem((4, 2, HALF, BLK), BF),
        vmem((4, HALF, HALF), BF),
        vmem((4, BLK, HALF), BF),
        vmem((2, 2, HALF, HALF), BF),
        vmem((HALF, n2), BF),
        vmem((2, HALF, HALF), BF),
        vmem((2, 2, HALF, HALF), BF),
        vmem((n2, HALF), BF),
        vmem((2, HALF, HALF), BF),
        vmem((2, 2, HALF, HALF), BF),
        vmem((4, HALF, HALF), BF),
        vmem((HALF, n2), BF),
        vmem((4, 2, HALF, BLK), BF),
        vmem((2, 2, P_SIZE, BLK), BF),
        vmem((n2, HALF), BF),
        vmem((2, 4, TH, HALF), BF),
        vmem((2, 4, TH, HALF), BF),
        vmem((2, 5, TH, HALF), F32),
        vmem((2, 5, TH, HALF), BF),
        vmem((2, 5, TH, HALF), BF),
        vmem((HALF + TH, HALF), BF),
        vmem((5, 4, TH, HALF), BF),
        vmem((5, 2, 4, TH, HALF), BF),
        vmem((2, 4, TH, HALF), F32),
        vmem((4, TH, HALF), BF), vmem((4, TH, HALF), BF),
        vmem((TH, HALF), BF), vmem((TH, HALF), BF),
        vmem((4, TH, HALF), BF), vmem((4, TH, HALF), BF),
        vmem((4, HALF, HALF), F32),
        dma((5,)), dma((4, 3)),
        dma((5,)), dma((SPAN + 1,)), dma((5,)), dma((2, 3)), dma((2, 4)), dma, dma, dma, dma,
        dma((2, 2)), dma((4,)), dma((5, 2)), dma((5,)), dma((2, 2)), dma((4,)),
        dma, dma, dma, dma,
        dma((4,)), dma((2, 2)), dma((5,)), dma((5, 2)), dma, dma, dma((2, 3)), dma((2, 4)),
        dma((2, 4)), dma((2, 4)), dma((2, 5)), dma((2, 5)),
    ]
    any_spec = pl.BlockSpec(memory_space=pl.ANY)
    return pl.pallas_call(
        functools.partial(body, tiles),
        out_shape=jax.ShapeDtypeStruct(object_slab.shape, F32),
        in_specs=[any_spec] * 7,
        out_specs=pl.BlockSpec(memory_space=pltpu.VMEM),
        scratch_shapes=scratch,
        compiler_params=pltpu.CompilerParams(
            collective_id=0, has_side_effects=True, vmem_limit_bytes=56_300_000
        ),
        name="object_gradient",
    )(row_offsets, position_counts, object_slab, probe_wave, amplitudes, near, far)


def solution(mesh):
    in_specs = (
        P(None, None, "tile", "scan"),
        P(None, None, "scan"),
        P("tile", "scan", None),
        P("tile"),
        P("tile"),
    )
    out_specs = P(None, None, "tile", "scan")
    far, near = tables()
    run = functools.partial(shards, mesh.shape["tile"], far, near)
    return jax.shard_map(run, mesh=mesh, in_specs=in_specs, out_specs=out_specs, check_vma=False)
```

```python
import functools
import math

import jax
import jax.numpy as jnp
import numpy as np
from jax import lax
from jax.experimental import pallas as pl
from jax.experimental.pallas import tpu as pltpu
from jax.sharding import PartitionSpec as P

P_SIZE = 512
HALF = 256
BLK = 128
TH = 64
SPAN = P_SIZE // TH

fresnel = 0.5
smooth = 1.0
MESH = pl.DeviceIdType.MESH
BF = jnp.bfloat16
F32 = jnp.float32


def tables():
    index = np.arange(P_SIZE)
    angles = 2.0 * np.pi / P_SIZE * (index[:, None] * index[None, :] % P_SIZE)
    wave = np.exp(1j * angles)
    far = np.conj(wave) / math.sqrt(P_SIZE)
    centred = np.where(index < P_SIZE // 2, index, index - P_SIZE).astype(np.float64)
    kernel = np.exp(-1j * np.pi * fresnel / P_SIZE * centred * centred)
    near = (wave * kernel[None, :]) @ np.conj(wave).T / P_SIZE

    def planes(table):
        both = np.stack([table.real, table.imag])
        return both.astype(np.float32).astype(BF)

    return planes(far), planes(near)


def body(
    tiles,
    off_hbm, cnt_hbm, slab_hbm, probe_hbm, amp_hbm, tq_hbm, tf_hbm,
    out_ref,
    off_ref, cnt_ref, slab, probe, ampf, aq, bq, af, bf,
    win, o2g, o2w, offb, sel, psel, put, h1, ampb, hr, o2r, amp,
    ps, ew, gs, x1, ch, ks, y, t2s, gw, b2s, b2r, tp, odd, got, even, outs, oin,
    pput, t2o, rin, acc, uo, ux, us, ui, xo, xi, mine,
    loc_sem, tab_sem,
    in_ss, in_rs, fw_ss, og_ss, og_rs, up_ss, up_rs, of_ss, of_rs,
    h1_ss, h1_rs, o2_ss, o2_rs, am_ss, am_rs,
    e1_ss, e1_rs, e2_ss, e2_rs, b2_ss, b2_rs, rt_ss, rt_rs, uu_ss, uu_rs, xs_ss, xs_rs, od_ss, od_rs, out_ss, out_rs,
):
    t = lax.axis_index("tile")
    x = lax.axis_index("scan")
    c = lax.rem(t, 2)
    d = 1 - c
    pair = t - c
    home = pair + lax.rem(x, 2)
    slot = x // 2
    odd_home = lax.rem(x, 2)
    row = lax.rem(t // 2, 4)
    plane = t - lax.rem(t, 8)

    def remote(src, dst, ss, rs, tile, scan):
        return pltpu.make_async_remote_copy(
            src_ref=src, dst_ref=dst, send_sem=ss, recv_sem=rs,
            device_id={"tile": tile, "scan": scan}, device_id_type=MESH,
        )

    loads = [
        pltpu.make_async_copy(slab_hbm, slab, loc_sem.at[0]),
        pltpu.make_async_copy(amp_hbm, ampf, loc_sem.at[1]),
        pltpu.make_async_copy(probe_hbm, probe, loc_sem.at[2]),
        pltpu.make_async_copy(off_hbm, off_ref, loc_sem.at[3]),
        pltpu.make_async_copy(cnt_hbm, cnt_ref, loc_sem.at[4]),
    ]
    for load in loads:
        load.start()

    barrier = pltpu.get_barrier_semaphore()

    def greet(tile, scan):
        pl.semaphore_signal(
            barrier, inc=1, device_id={"tile": tile, "scan": scan}, device_id_type=MESH
        )

    for n in range(1, 8):
        greet(plane + lax.rem(t + n, 8), x)
    def below(k):
        return t - k >= 0

    def above(k):
        return t + k < tiles

    for k in range(2, SPAN + 1, 2):
        @pl.when(above(k))
        def _():
            greet(t + k, x)

        @pl.when(below(k))
        def _():
            greet(t - k, x)
    for step in range(1, 4):
        for core in range(2):
            greet(pair + core, lax.rem(x + step, 4))

    def table_loads(src, dst, which, column):
        copies = []
        for n, (up, left, plane) in enumerate([(0, 0, 0), (1 - column, column, 1), (1, 1, 0)]):
            where = dst.at[pl.ds(up * P_SIZE, P_SIZE), pl.ds(left * P_SIZE, P_SIZE)]
            copies.append(pltpu.make_async_copy(src.at[plane], where, tab_sem.at[which, n]))
        for copy in copies:
            copy.start()
        return copies

    def table_ready(dst, copies, column):
        for copy in copies:
            copy.wait()
        imag = dst[(1 - column) * P_SIZE:(2 - column) * P_SIZE, column * P_SIZE:(column + 1) * P_SIZE]
        dst[column * P_SIZE:(column + 1) * P_SIZE, (1 - column) * P_SIZE:(2 - column) * P_SIZE] = -imag

    aq_loads = table_loads(tq_hbm, aq, 0, 0)
    bq_loads = table_loads(tq_hbm, bq, 1, 1)
    bf_loads = table_loads(tf_hbm, bf, 2, 1)
    af_loads = table_loads(tf_hbm, af, 3, 0)

    loads[0].wait()
    for part in range(2):
        win[0, :, part * BLK:(part + 1) * BLK] = slab[0, part].astype(BF)
        o2g[0, x, :, part * BLK:(part + 1) * BLK] = slab[1, part].astype(BF)
    loads[3].wait()
    loads[4].wait()
    shape = (8, 3 * BLK)
    offset = jnp.broadcast_to(off_ref[slot], shape)
    alive = jnp.broadcast_to(cnt_ref[0], shape) > jnp.broadcast_to(slot, shape)
    offb[c] = jnp.where(alive, offset, -2 * P_SIZE).astype(F32)

    for m in range(1, 5):
        @pl.when(jnp.logical_not(above(2 * m)))
        def _():
            win[2 * m] = jnp.zeros((TH, HALF), BF)

        @pl.when(jnp.logical_not(below(2 * m)))
        def _():
            oin[0, m] = jnp.zeros((TH, HALF), BF)

    @pl.when(jnp.logical_not(above(8)))
    def _():
        o2g[1, x] = jnp.zeros((TH, HALF), BF)

    @pl.when(jnp.logical_not(below(8)))
    def _():
        ui[...] = jnp.zeros((TH, HALF), BF)

    pl.semaphore_wait(
        barrier, 13 + jnp.minimum(4, (tiles - 1 - t) // 2) + jnp.minimum(4, t // 2))

    sends = []

    def start(copy, here=None):
        sends.append((copy, here))
        if here is None:
            copy.start()
        else:
            pl.when(here)(copy.start)

    def receive(dst, rs, here=None):
        copy = pltpu.make_async_copy(dst, dst, rs)
        if here is None:
            copy.wait()
        else:
            pl.when(here)(copy.wait)

    for k in range(2, SPAN + 1, 2):
        start(remote(
            win.at[0], win.at[k], in_ss.at[k // 2], in_rs.at[k], t - k, x), below(k))

    start(remote(o2g.at[0, x], o2g.at[1, x], up_ss, up_rs, t - 8, x), below(8))

    def pass_on(m):
        k = 2 * m - 1 + 2 * c
        return remote(win.at[2 * m], win.at[k], fw_ss.at[m], in_rs.at[k], pair + d, x)

    @pl.when(c == 1)
    def _():
        pass_on(0).start()

    def gather(source):
        for step in range(1, 4):
            start(remote(
                o2g.at[source, x], o2g.at[source, x], og_ss.at[source, step - 1],
                og_rs.at[source, x], t, lax.rem(x + step, 4)))

    def gathered(source):
        for step in range(1, 4):
            other = lax.rem(x + step, 4)
            receive(o2g.at[source, other], og_rs.at[source, other])

    gather(0)
    start(remote(offb.at[c], offb.at[c], of_ss, of_rs, pair + d, x))

    for s in range(2):
        shape = (P_SIZE, P_SIZE + TH)
        shifted = lax.broadcasted_iota(jnp.int32, shape, 0) + off_ref[s]
        match = shifted == lax.broadcasted_iota(jnp.int32, shape, 1)
        sel[s] = jnp.where(match, 1.0, 0.0).astype(BF)
    loads[1].wait()
    for s in range(2):
        for r in range(2):
            ampb[s, r] = ampf[s, :, r * HALF:(r + 1) * HALF].astype(BF)

    def is_self(s, r):
        return jnp.logical_and(2 * s + c == x, c == r)

    def spread(src, dst, ss, rs, s, r):
        mine = is_self(s, r)

        @pl.when(mine)
        def _():
            pltpu.make_async_copy(src, dst.at[x], rs.at[x]).start()

        @pl.when(jnp.logical_not(mine))
        def _():
            remote(src, dst.at[x], ss.at[s, r], rs.at[x], pair + r, 2 * s + c).start()

    def spread_wait(src, dst, ss, rs, s, r):
        @pl.when(jnp.logical_not(is_self(s, r)))
        def _():
            remote(src, dst.at[x], ss.at[s, r], rs.at[x], pair + r, 2 * s + c).wait_send()

    def amp_of(s, r):
        return ampb.at[s, r], amp, am_ss, am_rs, s, r

    def h1_of(s, r):
        return h1.at[s, :, pl.ds(r * HALF, HALF), :], hr, h1_ss, h1_rs, s, r

    for s in range(2):
        for r in range(2):
            spread(*amp_of(s, r))

    table_ready(aq, aq_loads, 0)
    table_ready(bq, bq_loads, 1)
    table_ready(bf, bf_loads, 1)
    table_ready(af, af_loads, 0)

    def plane_send(m, r, go, local):
        place = 2 * m + c - odd_home - 4 * r
        wanted = jnp.logical_and(place >= 0, place <= 4)
        for source in range(2):
            if m in (0, 4):
                if source != m // 4:
                    continue
                tile, here = pair + r, wanted
            else:
                tile = plane + 2 * lax.rem(row - m + 4, 4) + r
                here = jnp.logical_and(wanted, (m <= row) if source == 0 else (m > row))

            def copy():
                return remote(
                    o2g.at[source], o2w.at[place], o2_ss.at[m, r], o2_rs.at[place], tile, x)

            def own():
                return pltpu.make_async_copy(o2g.at[source], o2w.at[place], o2_rs.at[place])

            if source in go:
                if m in (0, 4):
                    @pl.when(jnp.logical_and(here, c != r))
                    def _():
                        copy().start() if local else copy().wait_send()

                    if local:
                        @pl.when(jnp.logical_and(here, c == r))
                        def _():
                            own().start()
                else:
                    @pl.when(here)
                    def _():
                        copy().start() if local else copy().wait_send()

    def take_tile(m, here, exists=None):
        receive(win.at[2 * m], in_rs.at[2 * m], here if exists is None else jnp.logical_and(here, exists))

        @pl.when(jnp.logical_and(here, jnp.logical_or(c == 0, m < 4)))
        def _():
            pass_on(m).start()

    for m in range(1, 4):
        take_tile(m, row + m <= 3)
    receive(o2g.at[1, x], up_rs, above(8))
    gather(1)
    for m in range(1, 5):
        take_tile(m, row + m > 3, above(2 * m))
    gathered(0)
    for m in range(4):
        for r in range(2):
            plane_send(m, r, (0,), True)

    def dot(left, right):
        return jnp.dot(left, right, preferred_element_type=F32)

    loads[2].wait()
    for k in range(1, SPAN + 1, 2):
        receive(win.at[k], in_rs.at[k])
    wide = jnp.concatenate([win[k] for k in range(SPAN + 1)], axis=0)
    psi = []
    for s in range(2):
        patch = dot(sel[s], wide)
        pr, pi = probe[0].astype(F32), probe[1].astype(F32)
        fr, fi = patch[:, :BLK], patch[:, BLK:]
        psi.append(jnp.concatenate([
            (pr * fr - pi * fi).astype(BF), (pr * fi + pi * fr).astype(BF)], axis=0))
    psi = jnp.concatenate(psi, axis=1)
    for r in range(2):
        for part in range(2):
            at = part * P_SIZE + r * HALF
            half1 = dot(aq[at:at + HALF, :], psi).astype(BF)
            for s in range(2):
                h1[s, part, r * HALF:(r + 1) * HALF, :] = half1[:, s * BLK:(s + 1) * BLK]
        for s in range(2):
            spread(*h1_of(s, r))

    gathered(1)
    for m in range(1, 5):
        for r in range(2):
            plane_send(m, r, (1,), True)

    for s in range(2):
        for b, k in enumerate((1, 3, 5, 7, 2, 4, 6, 8, 0)):
            shape = (TH, P_SIZE)
            shifted = lax.broadcasted_iota(jnp.int32, shape, 1) + off_ref[s]
            match = shifted == lax.broadcasted_iota(jnp.int32, shape, 0) + k * TH
            alive = jnp.broadcast_to(cnt_ref[0], shape) > s
            put[b * TH:(b + 1) * TH, s * P_SIZE:(s + 1) * P_SIZE] = jnp.where(
                jnp.logical_and(match, alive), 1.0, 0.0).astype(BF)
    receive(offb.at[d], of_rs)
    shape = (HALF, HALF + TH)
    shifted = lax.broadcasted_iota(jnp.int32, shape, 0).astype(F32) + offb[odd_home][0:1, :HALF + TH]
    match = shifted == lax.broadcasted_iota(jnp.int32, shape, 1).astype(F32)
    psel[...] = jnp.where(match, 1.0, 0.0).astype(BF)
    shape = (HALF + TH, HALF)
    shifted = lax.broadcasted_iota(jnp.int32, shape, 1).astype(F32) + offb[odd_home][0:1, :HALF]
    match = shifted == lax.broadcasted_iota(jnp.int32, shape, 0).astype(F32)
    pput[...] = jnp.where(match, 1.0, 0.0).astype(BF)
    acc[...] = jnp.zeros_like(acc)

    for n in range(4):
        receive(hr.at[n], h1_rs.at[n])
    left = jnp.concatenate([hr[n, part] for part in range(2) for n in range(4)], axis=1)
    for part in range(2):
        for h in range(2):
            at = part * P_SIZE + h * HALF
            ps[part, h] = dot(left, bq[:, at:at + HALF]).astype(BF)
    for k in range(5):
        receive(o2w.at[k], o2_rs.at[k])
    for n in range(4):
        rows = jnp.concatenate([o2w[k, n] for k in range(5)], axis=0)
        o2r[n] = dot(psel[...], rows).astype(BF)

    def second(part, h):
        columns = slice(part * BLK, (part + 1) * BLK)
        return jnp.concatenate([o2r[2 * h, :, columns], o2r[2 * h + 1, :, columns]], axis=1).astype(F32)

    for h in range(2):
        wr, wi = ps[0, h].astype(F32), ps[1, h].astype(F32)
        sr, si = second(0, h), second(1, h)
        ew[:, h * HALF:(h + 1) * HALF] = (wr * sr - wi * si).astype(BF)
        ew[:, P_SIZE + h * HALF:P_SIZE + (h + 1) * HALF] = (wr * si + wi * sr).astype(BF)

    for part in range(2):
        at = pl.multiple_of(part * P_SIZE + d * HALF, HALF)
        gs[part] = dot(ew[...], bf[:, pl.ds(at, HALF)]).astype(BF)
    ex1 = remote(gs, x1.at[c], e1_ss, e1_rs, pair + d, x)
    ex1.start()
    for part in range(2):
        at = pl.multiple_of(part * P_SIZE + c * HALF, HALF)
        x1[c, part] = dot(ew[...], bf[:, pl.ds(at, HALF)]).astype(BF)
    def near_rows(which, at):
        left = jnp.concatenate([
            af[at:at + HALF, pl.ds(pl.multiple_of(part * P_SIZE + which * HALF, HALF), HALF)]
            for part in range(2)], axis=1)
        return dot(left, jnp.concatenate([x1[which, part] for part in range(2)], axis=0))

    for n in range(4):
        mine[n] = near_rows(c, n * HALF)
    for n in range(4):
        receive(amp.at[n], am_rs.at[n])
    receive(x1.at[d], e1_rs)
    for r in range(2):
        fr = mine[r] + near_rows(d, r * HALF)
        fi = mine[2 + r] + near_rows(d, P_SIZE + r * HALF)
        measured = jnp.concatenate([amp[2 * r], amp[2 * r + 1]], axis=0).astype(F32)
        keeping = 1.0 - measured / jnp.sqrt(fr * fr + fi * fi + smooth)
        ch[r * HALF:(r + 1) * HALF, :] = (fr * keeping).astype(BF)
        ch[P_SIZE + r * HALF:P_SIZE + (r + 1) * HALF, :] = (fi * keeping).astype(BF)

    for part in range(2):
        at = pl.multiple_of(part * P_SIZE + d * HALF, HALF)
        ks[part] = dot(bf[pl.ds(at, HALF), :], ch[...]).astype(BF)
    ex2 = remote(ks, y.at[c], e2_ss, e2_rs, pair + d, x)
    ex2.start()
    for part in range(2):
        at = pl.multiple_of(part * P_SIZE + c * HALF, HALF)
        y[c, part] = dot(bf[pl.ds(at, HALF), :], ch[...]).astype(BF)
    def near_columns(which, at):
        right = jnp.concatenate([
            af[pl.ds(pl.multiple_of(part * P_SIZE + which * HALF, HALF), HALF), at:at + HALF]
            for part in range(2)], axis=0)
        return dot(jnp.concatenate([y[which, part] for part in range(2)], axis=1), right)

    for n in range(4):
        mine[n] = near_columns(c, n * HALF)
    receive(y.at[d], e2_rs)
    for h in range(2):
        er = mine[h] + near_columns(d, h * HALF)
        ei = mine[2 + h] + near_columns(d, P_SIZE + h * HALF)
        wr, wi = ps[0, h].astype(F32), ps[1, h].astype(F32)
        sr, si = second(0, h), second(1, h)
        tr, ti = (wr * er + wi * ei).astype(BF), (wr * ei - wi * er).astype(BF)
        for n in range(2):
            t2s[2 * h + n, :, :BLK] = tr[:, n * BLK:(n + 1) * BLK]
            t2s[2 * h + n, :, BLK:] = ti[:, n * BLK:(n + 1) * BLK]
        gw[:, h * HALF:(h + 1) * HALF] = (sr * er + si * ei).astype(BF)
        gw[:, P_SIZE + h * HALF:P_SIZE + (h + 1) * HALF] = (sr * ei - si * er).astype(BF)

    for n in range(4):
        moved = dot(pput[...], t2s[n]).astype(BF)
        for k in range(5):
            t2o[k, n] = moved[k * TH:(k + 1) * TH]

    def term_send(k, kind, begin):
        place = k + odd_home + 4 * c
        m = place // 2
        core = lax.rem(place, 2)
        tile = plane + 2 * lax.rem(row + m, 4) + core
        copy = remote(t2o.at[k], rin.at[m, c], rt_ss.at[k], rt_rs.at[m, c], tile, x)
        here = (row + m > 3) if kind else (row + m <= 3)

        @pl.when(jnp.logical_and(here, tile != t))
        def _():
            copy.start() if begin else copy.wait_send()

        if begin:
            @pl.when(jnp.logical_and(here, tile == t))
            def _():
                pltpu.make_async_copy(t2o.at[k], rin.at[m, c], rt_rs.at[m, c]).start()

    def term_take(m, r, kind):
        place = 2 * m + c - odd_home - 4 * r
        here = (m > row) if kind else (m <= row)

        @pl.when(jnp.logical_and(here, jnp.logical_and(place >= 0, place <= 4)))
        def _():
            receive(rin.at[m, r], rt_rs.at[m, r])
            acc[kind] += rin[m, r].astype(F32)

    for k in reversed(range(5)):
        term_send(k, 1, True)
    for k in reversed(range(5)):
        term_send(k, 0, True)

    def is_home(n):
        return jnp.logical_and(home == t, x == n)

    def give(src, dst, ss, rs, n):
        where = dst.at[slot, :, pl.ds(pl.multiple_of(c * HALF, HALF), HALF), :]

        @pl.when(is_home(n))
        def _():
            pltpu.make_async_copy(src.at[n], where, rs.at[slot, c]).start()

        @pl.when(jnp.logical_not(is_home(n)))
        def _():
            remote(src.at[n], where, ss.at[n], rs.at[slot, c], home, n).start()

    def give_wait(src, dst, ss, rs, n):
        where = dst.at[slot, :, pl.ds(pl.multiple_of(c * HALF, HALF), HALF), :]

        @pl.when(jnp.logical_not(is_home(n)))
        def _():
            remote(src.at[n], where, ss.at[n], rs.at[slot, c], home, n).wait_send()

    for h in range(2):
        for part in range(2):
            at = part * P_SIZE + h * HALF
            back2 = dot(gw[...], aq[:, at:at + HALF]).astype(BF)
            for n in range(2):
                b2s[2 * h + n, part] = back2[:, n * BLK:(n + 1) * BLK]
        for n in range(2):
            give(b2s, b2r, b2_ss, b2_rs, 2 * h + n)

    for s in range(2):
        for r in range(2):
            receive(b2r.at[s, :, pl.ds(r * HALF, HALF), :], b2_rs.at[s, r])
    right = jnp.concatenate([
        jnp.concatenate([b2r[0, part], b2r[1, part]], axis=1) for part in range(2)], axis=0)
    for r in range(2):
        nr = dot(bq[r * HALF:(r + 1) * HALF, :], right)
        ni = dot(bq[P_SIZE + r * HALF:P_SIZE + (r + 1) * HALF, :], right)
        pr = probe[0, r * HALF:(r + 1) * HALF, :].astype(F32)
        pi = probe[1, r * HALF:(r + 1) * HALF, :].astype(F32)
        for s in range(2):
            sr, si = nr[:, s * BLK:(s + 1) * BLK], ni[:, s * BLK:(s + 1) * BLK]
            rows = slice(s * P_SIZE + r * HALF, s * P_SIZE + (r + 1) * HALF)
            tp[rows, :BLK] = (pr * sr + pi * si).astype(BF)
            tp[rows, BLK:] = (pr * si - pi * sr).astype(BF)

    def collect(which, terms):
        total = dot(put[:HALF, :], terms)
        for m in range(4):
            odd[which, m] = total[m * TH:(m + 1) * TH].astype(BF)
            start(remote(
                odd.at[which, m], got.at[which, m], od_ss.at[which, m], od_rs.at[which, m],
                pair + d, x))
        total = dot(put[HALF:, :], terms)
        for m in range(1, 5):
            even[which, m] = total[(m - 1) * TH:m * TH]
        even[which, 0] = total[HALF:]

    def hand_on(which):
        for m in range(4):
            receive(got.at[which, m], od_rs.at[which, m])
            even[which, m + d] += got[which, m].astype(F32)
        for m in range(1, 5):
            outs[which, m] = even[which, m].astype(BF)
            start(remote(
                outs.at[which, m], oin.at[which, m], out_ss.at[which, m],
                out_rs.at[which, m], t + 2 * m, x), above(2 * m))

    collect(0, tp[...])
    for m in reversed(range(1, 5)):
        for r in range(2):
            term_take(m, r, 1)
    uo[...] = acc[1].astype(BF)
    for step in range(1, 4):
        other = lax.rem(x + step, 4)
        start(remote(uo.at[other], ux.at[x], xs_ss.at[1, step - 1], xs_rs.at[1, x], t, other))
    hand_on(0)
    for m in range(4):
        for r in range(2):
            term_take(m, r, 0)
    xo[...] = acc[0].astype(BF)
    for step in range(1, 4):
        other = lax.rem(x + step, 4)
        start(remote(xo.at[other], xi.at[x], xs_ss.at[0, step - 1], xs_rs.at[0, x], t, other))

    total = acc[1, x]
    for step in range(1, 4):
        other = lax.rem(x + step, 4)
        receive(ux.at[other], xs_rs.at[1, other])
        total = total + ux[other].astype(F32)
    us[...] = total.astype(BF)
    start(remote(us, ui, uu_ss, uu_rs, t + 8, x), above(8))

    total = even[0, 0]
    for m in range(1, 5):
        receive(oin.at[0, m], out_rs.at[0, m], below(2 * m))
        total = total + oin[0, m].astype(F32)
    for part in range(2):
        out_ref[0, part] = total[:, part * BLK:(part + 1) * BLK]

    total = acc[0, x]
    for step in range(1, 4):
        other = lax.rem(x + step, 4)
        receive(xi.at[other], xs_rs.at[0, other])
        total = total + xi[other].astype(F32)
    receive(ui, uu_rs, below(8))
    total = total + ui[...].astype(F32)
    for part in range(2):
        out_ref[1, part] = total[:, part * BLK:(part + 1) * BLK]

    for copy, here in sends:
        if here is None:
            copy.wait_send()
        else:
            pl.when(here)(copy.wait_send)
    for m in range(5):
        @pl.when((c == 1) if m == 0 else jnp.logical_or(c == 0, m < 4))
        def _():
            pass_on(m).wait_send()
        for r in range(2):
            plane_send(m, r, (0, 1), False)
    for k in range(5):
        term_send(k, 0, False)
        term_send(k, 1, False)
    ex1.wait_send()
    ex2.wait_send()
    for s in range(2):
        for r in range(2):
            spread_wait(*amp_of(s, r))
            spread_wait(*h1_of(s, r))
    for n in range(4):
        give_wait(b2s, b2r, b2_ss, b2_rs, n)


def shards(tiles, far, near, object_slab, probe_wave, amplitudes, row_offsets, position_counts):
    dma = pltpu.SemaphoreType.DMA
    vmem = pltpu.VMEM
    n2 = 2 * P_SIZE
    scratch = [
        pltpu.SMEM((2,), jnp.int32), pltpu.SMEM((1,), jnp.int32),
        vmem((2, 2, TH, BLK), F32),
        vmem((2, P_SIZE, BLK), BF),
        vmem((2, BLK, P_SIZE), F32),
        vmem((n2, n2), BF), vmem((n2, n2), BF), vmem((n2, n2), BF), vmem((n2, n2), BF),
        vmem((SPAN + 1, TH, HALF), BF),
        vmem((2, 4, TH, HALF), BF),
        vmem((5, 4, TH, HALF), BF),
        vmem((2, 8, 3 * BLK), F32),
        vmem((2, P_SIZE, P_SIZE + TH), BF),
        vmem((HALF, HALF + TH), BF),
        vmem((P_SIZE + TH, n2), BF),
        vmem((2, 2, P_SIZE, BLK), BF),
        vmem((2, 2, BLK, HALF), BF),
        vmem((4, 2, HALF, BLK), BF),
        vmem((4, HALF, HALF), BF),
        vmem((4, BLK, HALF), BF),
        vmem((2, 2, HALF, HALF), BF),
        vmem((HALF, n2), BF),
        vmem((2, HALF, HALF), BF),
        vmem((2, 2, HALF, HALF), BF),
        vmem((n2, HALF), BF),
        vmem((2, HALF, HALF), BF),
        vmem((2, 2, HALF, HALF), BF),
        vmem((4, HALF, HALF), BF),
        vmem((HALF, n2), BF),
        vmem((4, 2, HALF, BLK), BF),
        vmem((2, 2, P_SIZE, BLK), BF),
        vmem((n2, HALF), BF),
        vmem((2, 4, TH, HALF), BF),
        vmem((2, 4, TH, HALF), BF),
        vmem((2, 5, TH, HALF), F32),
        vmem((2, 5, TH, HALF), BF),
        vmem((2, 5, TH, HALF), BF),
        vmem((HALF + TH, HALF), BF),
        vmem((5, 4, TH, HALF), BF),
        vmem((5, 2, 4, TH, HALF), BF),
        vmem((2, 4, TH, HALF), F32),
        vmem((4, TH, HALF), BF), vmem((4, TH, HALF), BF),
        vmem((TH, HALF), BF), vmem((TH, HALF), BF),
        vmem((4, TH, HALF), BF), vmem((4, TH, HALF), BF),
        vmem((4, HALF, HALF), F32),
        dma((5,)), dma((4, 3)),
        dma((5,)), dma((SPAN + 1,)), dma((5,)), dma((2, 3)), dma((2, 4)), dma, dma, dma, dma,
        dma((2, 2)), dma((4,)), dma((5, 2)), dma((5,)), dma((2, 2)), dma((4,)),
        dma, dma, dma, dma,
        dma((4,)), dma((2, 2)), dma((5,)), dma((5, 2)), dma, dma, dma((2, 3)), dma((2, 4)),
        dma((2, 4)), dma((2, 4)), dma((2, 5)), dma((2, 5)),
    ]
    any_spec = pl.BlockSpec(memory_space=pl.ANY)
    return pl.pallas_call(
        functools.partial(body, tiles),
        out_shape=jax.ShapeDtypeStruct(object_slab.shape, F32),
        in_specs=[any_spec] * 7,
        out_specs=pl.BlockSpec(memory_space=pltpu.VMEM),
        scratch_shapes=scratch,
        compiler_params=pltpu.CompilerParams(
            collective_id=0, has_side_effects=True, vmem_limit_bytes=56_300_000
        ),
        name="object_gradient",
    )(row_offsets, position_counts, object_slab, probe_wave, amplitudes, near, far)


def solution(mesh):
    in_specs = (
        P(None, None, "tile", "scan"),
        P(None, None, "scan"),
        P("tile", "scan", None),
        P("tile"),
        P("tile"),
    )
    out_specs = P(None, None, "tile", "scan")
    far, near = tables()
    run = functools.partial(shards, mesh.shape["tile"], far, near)
    return jax.shard_map(run, mesh=mesh, in_specs=in_specs, out_specs=out_specs, check_vma=False)
```
